32 devices in a mesh: row: 2 (over x), col: 16 (over z, y, core).
Axes of the slice: x: 2, y: 2, z: 4, core: 2. Of those that a mesh axis runs over, the one named last changes fastest.
Arguments:
- pair_state: bfloat16 [256, 256, 256], P('row', 'col'), may hold values from -6 to 6
- residue_mask: int32 [256], replicated, may hold values 0 or 1
- chain_ids: int32 [256], replicated, may hold values from 0 to 3, never falling along the last dimension, each value on 1 to 128 neighbouring positions
- gain_transition: float32 [256], replicated, may hold values from 0.1 to 1.9
- hidden_weight: bfloat16 [256, 1024], replicated, may hold values from -0.375 to 0.375
- out_weight: bfloat16 [1024, 256], replicated, may hold values from -0.1875 to 0.1875
- gain_attention: float32 [256], replicated, may hold values from 0.1 to 1.9
- query_weight: bfloat16 [256, 256], replicated, may hold values from -4 to 4
- key_weight: bfloat16 [256, 256], replicated, may hold values from -4 to 4
- value_weight: bfloat16 [256, 256], replicated, may hold values from -0.375 to 0.375
- gate_weight: bfloat16 [256, 256], replicated, may hold values from -0.375 to 0.375
- bias_weight: bfloat16 [256, 8], replicated, may hold values from -0.375 to 0.375
- chain_weight: float32 [8], replicated, may hold values from -2 to 2
- output_weight: bfloat16 [256, 256], replicated, may hold values from -4 to 4
Outputs:
- symmetric_pair: bfloat16 [256, 256, 256], P('row', 'col')
The draws below stay inside these ranges and needn't reach their ends.
All inputs are finite; a program needn't handle non-finite values.
Results may differ from the reference program's by a relative error of at most 0.004.
The reference program's roundings to bfloat16 on the way (of `first_norm`, `hidden_act`, `normed`, `pair_bias`, `attn_weights`, `gated` and `update`) count: a program that leaves them out, or rounds other values in their place, can miss the bound.
Values may be sent and summed in bfloat16 or wider, within the bound.
A program may use at most 128 MiB of HBM per device.

```python
import math
import jax
import jax.numpy as jnp
import numpy as np
from jax import lax

PAIR_DIM = 256
HIDDEN_DIM = 1024
HEADS = 8
HEAD_DIM = 32
LENGTH = 256


def draw_query_weight(key, part):
    drawn = jax.random.normal(jax.random.fold_in(key, 21), (PAIR_DIM, HEADS * HEAD_DIM), jnp.float32) / math.sqrt(PAIR_DIM)
    return jnp.clip(drawn, -4.0, 4.0).astype(jnp.bfloat16)


def draw_key_weight(key, part):
    drawn = jax.random.normal(jax.random.fold_in(key, 23), (PAIR_DIM, HEADS * HEAD_DIM), jnp.float32) / math.sqrt(PAIR_DIM)
    return jnp.clip(drawn, -4.0, 4.0).astype(jnp.bfloat16)


def set_ends(values, stream_key, least, top_value):
    place = [jax.random.randint(jax.random.fold_in(stream_key, axis), (), 0, length) for axis, length in enumerate(values.shape)]
    longest = values.shape.index(max(values.shape))
    next_to = place[:longest] + [(place[longest] + 1) % values.shape[longest]] + place[longest + 1:]
    return values.at[tuple(place)].set(least).at[tuple(next_to)].set(top_value)


def block_levels(own_key, extent, shards, low, top_value):
    loudness, own = 1.0, jax.random.fold_in(own_key, 6)
    for dim, blocks in shards:
        heights = jnp.exp(jax.random.uniform(jax.random.fold_in(own, dim), (blocks,), jnp.float32, low / len(shards), top_value / len(shards)))
        loudness = loudness * jnp.repeat(heights, extent[dim] // blocks).reshape([-1 if axis == dim else 1 for axis in range(len(extent))])
    return loudness


def profile(amount, total, limit, lean):
    weights = [(1 << 20) // math.isqrt(rank ** lean) + 1 for rank in range(2, amount + 1)]
    spare, holding = total - limit - (amount - 1), [1] * (amount - 1)
    while spare > 0:
        candidates = [i for i in range(amount - 1) if holding[i] < limit]
        pool, budget = sum([weights[i] for i in candidates]), spare
        for i in candidates:
            extra = min(limit - holding[i], max(1, budget * weights[i] // pool), spare)
            holding[i] = holding[i] + extra
            spare = spare - extra
    return np.array([limit] + holding)


def uneven_parts(key, amount, total, bound, slope):
    if amount == 2:
        one = jax.random.randint(key, (), max(1, total - bound), min(bound, total - 1) + 1)
        return jnp.stack([one, total - one])
    tallies = jnp.asarray(profile(amount, total, bound, slope), jnp.int32)
    couples = (amount - 1) // 2
    source_of, receiver = tallies[1:1 + 2 * couples:2], tallies[2:2 + 2 * couples:2]
    slack = jnp.minimum(source_of - 1, bound - receiver)
    moved = jax.random.randint(jax.random.fold_in(key, 1), (couples,), 0, 1 << 20) % (slack + 1)
    tallies = tallies.at[1:1 + 2 * couples:2].set(source_of - moved).at[2:2 + 2 * couples:2].set(receiver + moved)
    return tallies[jax.random.permutation(jax.random.fold_in(key, 2), amount)]


def bell_draw(stream_key, extent, spread, reach, cuts=(), kind=jnp.bfloat16):
    entries = spread * jax.random.normal(stream_key, extent, jnp.float32)
    if cuts:
        entries = entries * block_levels(stream_key, extent, cuts, -0.22, 0.18)
    return jnp.clip(entries, -reach, reach).astype(kind)


def setup_inputs(seed: int = 0) -> dict:
    seeds = jax.random.split(jax.random.key(seed), 15)
    return {
        "pair_state": bell_draw(seeds[0], (LENGTH, LENGTH, PAIR_DIM), 1.0, 6.0, ((0, 2), (1, 16))),
        "residue_mask": set_ends((jax.random.randint(seeds[1], (LENGTH,), 0, 4) < 3).astype(jnp.int32), jax.random.fold_in(seeds[1], 1), 0, 1),
        "chain_ids": jnp.searchsorted(jnp.cumsum(uneven_parts(seeds[2], 4, LENGTH, LENGTH // 2, 0)), jnp.arange(LENGTH), side="right").astype(jnp.int32),
        "gain_transition": jnp.clip(1.0 + 0.18 * jax.random.normal(seeds[3], (PAIR_DIM,), jnp.float32), 0.1, 1.9),
        "hidden_weight": bell_draw(seeds[4], (PAIR_DIM, HIDDEN_DIM), PAIR_DIM ** -0.5, 0.375),
        "out_weight": bell_draw(seeds[5], (HIDDEN_DIM, PAIR_DIM), HIDDEN_DIM ** -0.5, 0.1875),
        "gain_attention": jnp.clip(1.0 + 0.18 * jax.random.normal(seeds[6], (PAIR_DIM,), jnp.float32), 0.1, 1.9),
        "query_weight": draw_query_weight(jax.random.fold_in(seeds[14], 71), 0),
        "key_weight": draw_key_weight(jax.random.fold_in(seeds[14], 71), 0),
        "value_weight": bell_draw(seeds[9], (PAIR_DIM, HEADS * HEAD_DIM), PAIR_DIM ** -0.5, 0.375),
        "gate_weight": bell_draw(seeds[10], (PAIR_DIM, HEADS * HEAD_DIM), PAIR_DIM ** -0.5, 0.375),
        "bias_weight": bell_draw(seeds[11], (PAIR_DIM, HEADS), PAIR_DIM ** -0.5, 0.375),
        "chain_weight": jnp.clip(jax.random.uniform(seeds[12], (HEADS,), jnp.float32, -2.0, 2.0), -2.0, 2.0),
        "output_weight": bell_draw(seeds[13], (HEADS * HEAD_DIM, PAIR_DIM), 0.25, 4.0),
    }


mask_penalty = 1000000000.0
norm_epsilon = 1e-05

def normalize(values, gain):
    center = values - lax.optimization_barrier(jnp.mean(values, axis=-1, keepdims=True))
    variance = lax.optimization_barrier(jnp.mean(center * center, axis=-1, keepdims=True))
    return center * lax.rsqrt(variance + norm_epsilon) * gain

def reference(pair_state, residue_mask, chain_ids, gain_transition, hidden_weight, out_weight, gain_attention, query_weight, key_weight, value_weight, gate_weight, bias_weight, chain_weight, output_weight):
    length = pair_state.shape[0]
    head_count = chain_weight.shape[0]
    head_dim = query_weight.shape[1] // head_count
    score_scale = 1.0 / math.sqrt(head_dim)
    positions = jnp.arange(length, dtype=jnp.int32)

    def transition_row(position):
        sym_row = pair_state[position].astype(jnp.float32) + pair_state[:, position].astype(jnp.float32)
        first_norm = normalize(sym_row, gain_transition).astype(jnp.bfloat16)
        hidden_act = jax.nn.relu(jnp.dot(first_norm, hidden_weight, preferred_element_type=jnp.float32)).astype(jnp.bfloat16)
        carried_row = sym_row + jnp.dot(hidden_act, out_weight, preferred_element_type=jnp.float32)
        normed_row = normalize(carried_row, gain_attention).astype(jnp.bfloat16)
        return (carried_row, normed_row)
    carried, normed = lax.map(transition_row, positions)

    def bias_row(normed_row):
        return jnp.dot(normed_row, bias_weight, preferred_element_type=jnp.float32).astype(jnp.bfloat16)
    pair_bias = jnp.transpose(lax.map(bias_row, normed), (2, 0, 1)).astype(jnp.float32)
    same_chain = (chain_ids[:, None] == chain_ids[None, :]).astype(jnp.float32)
    penalty = mask_penalty * (1 - residue_mask).astype(jnp.float32)
    full_bias = pair_bias + chain_weight[:, None, None] * same_chain[None] - penalty[None, None, :]

    def attend_row(normed_row):
        query_rows = jnp.dot(normed_row, query_weight, preferred_element_type=jnp.float32).astype(jnp.bfloat16).reshape(length, head_count, head_dim)
        key_rows = jnp.dot(normed_row, key_weight, preferred_element_type=jnp.float32).astype(jnp.bfloat16).reshape(length, head_count, head_dim)
        value_rows = jnp.dot(normed_row, value_weight, preferred_element_type=jnp.float32).astype(jnp.bfloat16).reshape(length, head_count, head_dim)
        gate_vals = jax.nn.sigmoid(jnp.dot(normed_row, gate_weight, preferred_element_type=jnp.float32))
        scores = jnp.einsum('jhd,khd->hjk', query_rows.astype(jnp.float32), key_rows.astype(jnp.float32)) * score_scale + full_bias
        row_max = lax.optimization_barrier(jnp.max(scores, axis=-1, keepdims=True))
        exponent = jnp.exp(scores - row_max)
        attn_weights = (exponent / lax.optimization_barrier(jnp.sum(exponent, axis=-1, keepdims=True))).astype(jnp.bfloat16)
        mixture = jnp.einsum('hjk,khd->jhd', attn_weights.astype(jnp.float32), value_rows.astype(jnp.float32)).reshape(length, head_count * head_dim)
        gated = (gate_vals * mixture).astype(jnp.bfloat16)
        return jnp.dot(gated, output_weight, preferred_element_type=jnp.float32).astype(jnp.bfloat16)
    update = lax.map(attend_row, normed)
    layer_out = carried + update.astype(jnp.float32)
    return (layer_out + jnp.swapaxes(layer_out, 0, 1)).astype(jnp.bfloat16)
```

```python
import functools
import math

import jax
import jax.numpy as jnp
from jax import lax
from jax.experimental import pallas as pl
from jax.experimental.pallas import tpu as pltpu
from jax.sharding import PartitionSpec as P

MESH = pl.DeviceIdType.MESH
VMEM_LIMIT = 60 * 1024 * 1024

mask_penalty = 1000000000.0
norm_epsilon = 1e-05


def normalize(values, gain):
    center = values - jnp.mean(values, axis=-1, keepdims=True)
    variance = jnp.mean(center * center, axis=-1, keepdims=True)
    return center * lax.rsqrt(variance + norm_epsilon) * gain


def mirror(tile):
    tile_rows, tile_cols, channels = tile.shape
    col_count = lax.axis_size("col")
    row_count = lax.axis_size("row")
    col_ratio = col_count // row_count
    piece_len = tile_cols * tile_cols // col_count
    sectioned = tile.reshape(col_ratio, col_count, piece_len, channels)
    sectioned = lax.all_to_all(sectioned, "col", split_axis=1, concat_axis=1, tiled=True)
    sectioned = sectioned.reshape(col_ratio, row_count, col_ratio, piece_len, channels)
    sectioned = lax.all_to_all(sectioned, "row", split_axis=1, concat_axis=1, tiled=True)
    sectioned = jnp.transpose(sectioned, (1, 0, 2, 3, 4)).reshape(
        col_count, col_ratio, piece_len, channels
    )
    sectioned = lax.all_to_all(sectioned, "col", split_axis=0, concat_axis=0, tiled=True)
    sectioned = jnp.transpose(sectioned, (1, 0, 2, 3)).reshape(
        col_ratio, tile_cols, tile_cols, channels
    )
    return jnp.transpose(sectioned, (0, 2, 1, 3)).reshape(tile_rows, tile_cols, channels)


def attend(query_part, gate_part, key_part, value_part, bias_part, head_count, output_weight):
    query_total = query_part.shape[0]
    key_total = key_part.shape[0]
    head_dim = query_part.shape[1] // head_count
    score_scale = 1.0 / math.sqrt(head_dim)
    query_heads = query_part.reshape(query_total, head_count, head_dim)
    key_heads = key_part.reshape(key_total, head_count, head_dim)
    value_heads = value_part.reshape(key_total, head_count, head_dim)
    scores = (
        jnp.einsum("jhd,khd->hjk", query_heads, key_heads, preferred_element_type=jnp.float32)
        * score_scale
        + bias_part
    )
    row_max = jnp.max(scores, axis=-1, keepdims=True)
    exponent = jnp.exp(scores - row_max)
    attn_weights = (exponent / jnp.sum(exponent, axis=-1, keepdims=True)).astype(jnp.bfloat16)
    mixture = jnp.einsum(
        "hjk,khd->jhd", attn_weights, value_heads, preferred_element_type=jnp.float32
    )
    gated = (gate_part * mixture.reshape(query_total, head_count * head_dim)).astype(jnp.bfloat16)
    return jnp.dot(gated, output_weight, preferred_element_type=jnp.float32).astype(jnp.bfloat16)


def mirror_layout(
    normed_tile,
    bias_tile,
    chain_ids,
    penalty,
    chain_weight,
    query_weight,
    key_weight,
    value_weight,
    gate_weight,
    output_weight,
):
    tile_rows, tile_cols, channels = normed_tile.shape
    head_count = bias_tile.shape[0]
    row_start = lax.axis_index("row") * tile_rows
    flat_tile = normed_tile.reshape(tile_rows * tile_cols, channels)
    key_tile = (
        jnp.dot(flat_tile, key_weight, preferred_element_type=jnp.float32)
        .astype(jnp.bfloat16)
        .reshape(tile_rows, tile_cols, -1)
    )
    value_tile = (
        jnp.dot(flat_tile, value_weight, preferred_element_type=jnp.float32)
        .astype(jnp.bfloat16)
        .reshape(tile_rows, tile_cols, -1)
    )
    key_all, value_all = (
        lax.all_gather(key_tile, "row", axis=0, tiled=True),
        lax.all_gather(value_tile, "row", axis=0, tiled=True),
    )
    bias_rows = lax.all_gather(bias_tile, "col", axis=2, tiled=True)
    chain_rows = lax.dynamic_slice_in_dim(chain_ids, row_start, tile_rows, 0)
    same_chain = (chain_rows[:, None] == chain_ids[None, :]).astype(jnp.float32)
    bias_full = (
        bias_rows.astype(jnp.float32)
        + chain_weight[:, None, None] * same_chain[None]
        - penalty[None, None, :]
    )
    query_tile = (
        jnp.dot(flat_tile, query_weight, preferred_element_type=jnp.float32)
        .astype(jnp.bfloat16)
        .reshape(tile_rows, tile_cols, -1)
    )
    gate_tile = jax.nn.sigmoid(
        jnp.dot(flat_tile, gate_weight, preferred_element_type=jnp.float32)
    ).reshape(tile_rows, tile_cols, -1)

    def one_column(position):
        query_part = lax.dynamic_index_in_dim(query_tile, position, 1, keepdims=False)
        gate_part = lax.dynamic_index_in_dim(gate_tile, position, 1, keepdims=False)
        key_part = lax.dynamic_index_in_dim(key_all, position, 1, keepdims=False)
        value_part = lax.dynamic_index_in_dim(value_all, position, 1, keepdims=False)
        return attend(
            query_part, gate_part, key_part, value_part, bias_full, head_count, output_weight
        )

    results = lax.map(one_column, jnp.arange(tile_cols, dtype=jnp.int32))
    return jnp.transpose(results, (1, 0, 2))


def tile_layout(
    pair_state,
    residue_mask,
    chain_ids,
    gain_transition,
    hidden_weight,
    out_weight,
    gain_attention,
    query_weight,
    key_weight,
    value_weight,
    gate_weight,
    bias_weight,
    chain_weight,
    output_weight,
):
    tile_rows, tile_cols, channels = pair_state.shape
    head_count = chain_weight.shape[0]
    mirrored = mirror(pair_state)
    sym_tile = pair_state.astype(jnp.float32) + mirrored.astype(jnp.float32)
    flat_sym = sym_tile.reshape(tile_rows * tile_cols, channels)
    first_norm = normalize(flat_sym, gain_transition).astype(jnp.bfloat16)
    hidden_act = jax.nn.relu(
        jnp.dot(first_norm, hidden_weight, preferred_element_type=jnp.float32)
    ).astype(jnp.bfloat16)
    carried = flat_sym + jnp.dot(hidden_act, out_weight, preferred_element_type=jnp.float32)
    normed = normalize(carried, gain_attention).astype(jnp.bfloat16)
    bias_tile = (
        jnp.einsum("pd,dh->hp", normed, bias_weight, preferred_element_type=jnp.float32)
        .astype(jnp.bfloat16)
        .reshape(head_count, tile_rows, tile_cols)
    )
    penalty = mask_penalty * (1 - residue_mask).astype(jnp.float32)
    normed_tile = normed.reshape(tile_rows, tile_cols, channels)
    arguments = (
        normed_tile,
        bias_tile,
        chain_ids,
        penalty,
        chain_weight,
        query_weight,
        key_weight,
        value_weight,
        gate_weight,
        output_weight,
    )
    own_update = mirror_layout(*arguments)
    other_update = mirror(own_update)
    total = (
        2.0 * carried.reshape(tile_rows, tile_cols, channels)
        + own_update.astype(jnp.float32)
        + other_update.astype(jnp.float32)
    )
    return total.astype(jnp.bfloat16)


def greet_all(row_count, col_count):
    device_total = row_count * col_count
    me = lax.axis_index("col") * row_count + lax.axis_index("row")
    barrier = pltpu.get_barrier_semaphore()

    def greet(step, carry):
        peer = lax.rem(me + step, device_total)
        pl.semaphore_signal(
            barrier,
            inc=1,
            device_id=(lax.rem(peer, row_count), peer // row_count),
            device_id_type=MESH,
        )
        return carry

    lax.fori_loop(1, device_total, greet, 0)
    pl.semaphore_wait(barrier, device_total - 1)


def transition_kernel(
    row_count,
    col_count,
    tile_ref,
    turned_ref,
    gain_transition_ref,
    hidden_weight_ref,
    out_weight_ref,
    gain_attention_ref,
    bias_weight_ref,
    carried_ref,
    normed_ref,
    bias_ref,
    row_buf,
    col_buf,
    row_send,
    row_recv,
    col_send,
    col_recv,
    bias_send,
    bias_recv,
):
    tile_rows, tile_cols, channels = tile_ref.shape
    own = tile_cols // row_count
    groups = tile_rows // own
    device_total = row_count * col_count
    row_id, col_id = lax.axis_index("row"), lax.axis_index("col")
    me = col_id * row_count + row_id
    greet_all(row_count, col_count)

    def row_copy(group):
        target = row_id * groups + group
        source = tile_ref.at[pl.ds(group * own, own)]
        landing = row_buf.at[:, pl.ds(pl.multiple_of(col_id * tile_cols, tile_cols), tile_cols), :]
        return target, source, landing

    def row_remote(group):
        target, source, landing = row_copy(group)
        return pltpu.make_async_remote_copy(
            src_ref=source,
            dst_ref=landing,
            send_sem=row_send.at[group],
            recv_sem=row_recv.at[col_id],
            device_id=(lax.rem(target, row_count), target // row_count),
            device_id_type=MESH,
        )

    def row_local(group):
        target, source, landing = row_copy(group)
        return pltpu.make_async_copy(source, landing, row_recv.at[col_id])

    def col_remote(other):
        return pltpu.make_async_remote_copy(
            src_ref=turned_ref.at[pl.ds(other * own, own)],
            dst_ref=col_buf.at[
                :, pl.ds(pl.multiple_of(row_id * tile_rows, tile_rows), tile_rows), :
            ],
            send_sem=col_send.at[other],
            recv_sem=col_recv.at[row_id],
            device_id=(other, col_id),
            device_id_type=MESH,
        )

    def start_row(step, carry):
        group = lax.rem(step + me, groups)
        target = row_id * groups + group

        @pl.when(target != me)
        def _():
            row_remote(group).start()

        @pl.when(target == me)
        def _():
            row_local(group).start()

        return carry

    lax.fori_loop(0, groups, start_row, 0)

    def start_col(step, carry):
        col_remote(lax.rem(row_id + step, row_count)).start()
        return carry

    lax.fori_loop(1, row_count, start_col, 0)
    own_col = pltpu.make_async_copy(
        turned_ref.at[pl.ds(row_id * own, own)],
        col_buf.at[:, pl.ds(pl.multiple_of(row_id * tile_rows, tile_rows), tile_rows), :],
        col_recv.at[row_id],
    )
    own_col.start()

    def wait_row(other, carry):
        landed = row_buf.at[:, pl.ds(pl.multiple_of(other * tile_cols, tile_cols), tile_cols), :]
        pltpu.make_async_copy(landed, landed, row_recv.at[other]).wait()
        return carry

    lax.fori_loop(0, col_count, wait_row, 0)

    def wait_col(other, carry):
        landed = col_buf.at[:, pl.ds(pl.multiple_of(other * tile_rows, tile_rows), tile_rows), :]
        pltpu.make_async_copy(landed, landed, col_recv.at[other]).wait()
        return carry

    lax.fori_loop(0, row_count, wait_col, 0)

    def one_row(position, carry):
        sym_row = row_buf[position].astype(jnp.float32) + col_buf[position].astype(jnp.float32)
        first_norm = normalize(sym_row, gain_transition_ref[...]).astype(jnp.bfloat16)
        hidden_act = jax.nn.relu(
            jnp.dot(first_norm, hidden_weight_ref[...], preferred_element_type=jnp.float32)
        ).astype(jnp.bfloat16)
        carried = sym_row + jnp.dot(
            hidden_act, out_weight_ref[...], preferred_element_type=jnp.float32
        )
        carried_ref[position] = carried
        normed = normalize(carried, gain_attention_ref[...]).astype(jnp.bfloat16)
        normed_ref[position] = normed
        bias_ref[me * own + position] = lax.dot_general(
            bias_weight_ref[...],
            normed,
            (((1,), (1,)), ((), ())),
            preferred_element_type=jnp.float32,
        ).astype(jnp.bfloat16)
        return carry

    lax.fori_loop(0, own, one_row, 0)

    def bias_remote(peer):
        return pltpu.make_async_remote_copy(
            src_ref=bias_ref.at[pl.ds(me * own, own)],
            dst_ref=bias_ref.at[pl.ds(me * own, own)],
            send_sem=bias_send.at[peer],
            recv_sem=bias_recv.at[me],
            device_id=(lax.rem(peer, row_count), peer // row_count),
            device_id_type=MESH,
        )

    def start_bias(step, carry):
        bias_remote(lax.rem(me + step, device_total)).start()
        return carry

    lax.fori_loop(1, device_total, start_bias, 0)

    def wait_bias(step, carry):
        peer = lax.rem(me + step, device_total)
        landed = bias_ref.at[pl.ds(peer * own, own)]
        pltpu.make_async_copy(landed, landed, bias_recv.at[peer]).wait()
        bias_remote(peer).wait_send()
        return carry

    lax.fori_loop(1, device_total, wait_bias, 0)

    def finish_row(group, carry):
        @pl.when(row_id * groups + group != me)
        def _():
            row_remote(group).wait_send()

        return carry

    lax.fori_loop(0, groups, finish_row, 0)

    def finish_col(step, carry):
        col_remote(lax.rem(row_id + step, row_count)).wait_send()
        return carry

    lax.fori_loop(1, row_count, finish_col, 0)


def attention_kernel(
    row_count,
    col_count,
    carried_ref,
    normed_ref,
    bias_ref,
    query_weight_ref,
    key_weight_ref,
    value_weight_ref,
    gate_weight_ref,
    output_weight_ref,
    out_ref,
    total,
    update_buf,
    recv_buf,
    turned,
    sum_buf,
    update_send,
    update_recv,
    sum_send,
    sum_recv,
):
    own, length, channels = normed_ref.shape
    head_count = bias_ref.shape[0]
    head_dim = query_weight_ref.shape[1] // head_count
    score_scale = 1.0 / math.sqrt(head_dim)
    tile_rows = length // row_count
    device_total = row_count * col_count
    row_id, col_id = lax.axis_index("row"), lax.axis_index("col")
    me = col_id * row_count + row_id
    greet_all(row_count, col_count)

    def update_remote(position, peer):
        return pltpu.make_async_remote_copy(
            src_ref=update_buf.at[position, peer],
            dst_ref=recv_buf.at[me * own + position],
            send_sem=update_send.at[peer],
            recv_sem=update_recv.at[me],
            device_id=(lax.rem(peer, row_count), peer // row_count),
            device_id_type=MESH,
        )

    head_of_lane = lax.broadcasted_iota(jnp.int32, (1, channels), 1) // head_dim

    def one_row(position, carry):
        normed = normed_ref[position]

        def project(weight_ref):
            return jnp.dot(normed, weight_ref[...], preferred_element_type=jnp.float32)

        queries = project(query_weight_ref).astype(jnp.bfloat16)
        keys_turned = project(key_weight_ref).astype(jnp.bfloat16).T
        values = project(value_weight_ref).astype(jnp.bfloat16)
        gates = jax.nn.sigmoid(project(gate_weight_ref))
        mixture = jnp.zeros((length, channels), jnp.float32)
        for head in range(head_count):
            chosen = (head_of_lane == head).astype(jnp.bfloat16)
            scores = (
                jnp.dot(queries * chosen, keys_turned, preferred_element_type=jnp.float32)
                * score_scale
                + bias_ref[head]
            )
            row_max = jnp.max(scores, axis=-1, keepdims=True)
            exponent = jnp.exp(scores - row_max)
            attn_weights = (
                exponent * (1.0 / jnp.sum(exponent, axis=-1, keepdims=True))
            ).astype(jnp.bfloat16)
            mixture = mixture + jnp.dot(
                attn_weights, values * chosen, preferred_element_type=jnp.float32
            )
        gated = (gates * mixture).astype(jnp.bfloat16)
        update = jnp.dot(gated, output_weight_ref[...], preferred_element_type=jnp.float32)
        update = update.reshape(device_total, own, channels).astype(jnp.bfloat16)
        update_buf[position] = update
        recv_buf[me * own + position] = update_buf[position, me]
        total[position] = 2.0 * carried_ref[position] + update.astype(jnp.float32).reshape(
            length, channels
        )

        def send(step, inner):
            update_remote(position, lax.rem(me + step, device_total)).start()
            return inner

        lax.fori_loop(1, device_total, send, 0)
        return carry

    lax.fori_loop(0, own, one_row, 0)
    for position in range(own):
        turned[:, position, :] = total[position]

    def wait_update(step, carry):
        peer = lax.rem(me + step, device_total)
        landed = recv_buf.at[pl.ds(peer * own, own)]
        pltpu.make_async_copy(landed, landed, update_recv.at[peer]).wait()
        pltpu.make_async_copy(landed, landed, update_send.at[peer]).wait()
        return carry

    lax.fori_loop(1, device_total, wait_update, 0)

    def sum_remote(other):
        return pltpu.make_async_remote_copy(
            src_ref=sum_buf.at[other],
            dst_ref=out_ref.at[row_id],
            send_sem=sum_send.at[other],
            recv_sem=sum_recv.at[row_id],
            device_id=(other, col_id),
            device_id_type=MESH,
        )

    def sum_rows(other, target_ref):
        def one_block(block, carry):
            rows = pl.ds(other * tile_rows + block * own, own)
            summed = turned[rows] + recv_buf[rows].astype(jnp.float32)
            target_ref[other, pl.ds(block * own, own)] = summed.astype(jnp.bfloat16)
            return carry

        lax.fori_loop(0, tile_rows // own, one_block, 0)

    def send_sum(step, carry):
        other = lax.rem(row_id + step, row_count)
        sum_rows(other, sum_buf)
        sum_remote(other).start()
        return carry

    lax.fori_loop(1, row_count, send_sum, 0)
    sum_rows(row_id, out_ref)

    def wait_sum(step, carry):
        other = lax.rem(row_id + step, row_count)
        landed = out_ref.at[other]
        pltpu.make_async_copy(landed, landed, sum_recv.at[other]).wait()
        sum_remote(other).wait_send()
        return carry

    lax.fori_loop(1, row_count, wait_sum, 0)


def owned_columns(
    pair_state,
    residue_mask,
    chain_ids,
    gain_transition,
    hidden_weight,
    out_weight,
    gain_attention,
    query_weight,
    key_weight,
    value_weight,
    gate_weight,
    bias_weight,
    chain_weight,
    output_weight,
):
    tile_rows, tile_cols, channels = pair_state.shape
    row_count, col_count = lax.axis_size("row"), lax.axis_size("col")
    device_total = row_count * col_count
    head_count = chain_weight.shape[0]
    length = tile_rows * row_count
    own = tile_cols // row_count
    in_vmem = pl.BlockSpec(memory_space=pltpu.VMEM)
    dma = pltpu.SemaphoreType.DMA
    carried, normed, bias_rows = pl.pallas_call(
        functools.partial(transition_kernel, row_count, col_count),
        out_shape=(
            jax.ShapeDtypeStruct((own, length, channels), jnp.float32),
            jax.ShapeDtypeStruct((own, length, channels), jnp.bfloat16),
            jax.ShapeDtypeStruct((length, head_count, length), jnp.bfloat16),
        ),
        in_specs=[in_vmem] * 7,
        out_specs=(in_vmem,) * 3,
        scratch_shapes=[
            pltpu.VMEM((own, length, channels), jnp.bfloat16),
            pltpu.VMEM((own, length, channels), jnp.bfloat16),
            dma((tile_rows // own,)),
            dma((col_count,)),
            dma((row_count,)),
            dma((row_count,)),
            dma((device_total,)),
            dma((device_total,)),
        ],
        compiler_params=pltpu.CompilerParams(
            collective_id=0, has_side_effects=True, vmem_limit_bytes=VMEM_LIMIT
        ),
        name="transition",
    )(
        pair_state,
        jnp.transpose(pair_state, (1, 0, 2)),
        gain_transition[None, :],
        hidden_weight,
        out_weight,
        gain_attention[None, :],
        bias_weight.T,
    )
    penalty = mask_penalty * (1 - residue_mask).astype(jnp.float32)
    same_chain = (chain_ids[:, None] == chain_ids[None, :]).astype(jnp.float32)
    bias_full = (
        jnp.transpose(bias_rows, (1, 0, 2)).astype(jnp.float32)
        + chain_weight[:, None, None] * same_chain[None]
        - penalty[None, None, :]
    )
    pieces = pl.pallas_call(
        functools.partial(attention_kernel, row_count, col_count),
        out_shape=jax.ShapeDtypeStruct((row_count, tile_rows, own, channels), jnp.bfloat16),
        in_specs=[in_vmem] * 8,
        out_specs=in_vmem,
        scratch_shapes=[
            pltpu.VMEM((own, length, channels), jnp.float32),
            pltpu.VMEM((own, device_total, own, channels), jnp.bfloat16),
            pltpu.VMEM((length, own, channels), jnp.bfloat16),
            pltpu.VMEM((length, own, channels), jnp.float32),
            pltpu.VMEM((row_count, tile_rows, own, channels), jnp.bfloat16),
            dma((device_total,)),
            dma((device_total,)),
            dma((row_count,)),
            dma((row_count,)),
        ],
        compiler_params=pltpu.CompilerParams(
            collective_id=1, has_side_effects=True, vmem_limit_bytes=VMEM_LIMIT
        ),
        name="attention",
    )(
        carried,
        normed,
        bias_full,
        query_weight,
        key_weight,
        value_weight,
        gate_weight,
        output_weight,
    )
    return jnp.transpose(pieces, (1, 0, 2, 3)).reshape(tile_rows, tile_cols, channels)


def per_device(pair_state, *others):
    tile_cols = pair_state.shape[1]
    row_count = lax.axis_size("row")
    own = tile_cols // row_count
    if own % 8 == 0:
        return owned_columns(pair_state, *others)
    return tile_layout(pair_state, *others)


def solution(mesh):
    placed = (
        P("row", "col", None),
        P(),
        P(),
        P(),
        P(),
        P(),
        P(),
        P(),
        P(),
        P(),
        P(),
        P(),
        P(),
        P(),
    )
    return jax.shard_map(
        per_device, mesh=mesh, in_specs=placed, out_specs=P("row", "col", None), check_vma=False
    )
```

```python
import functools
import math

import jax
import jax.numpy as jnp
from jax import lax
from jax.experimental import pallas as pl
from jax.experimental.pallas import tpu as pltpu
from jax.sharding import PartitionSpec as P

MESH = pl.DeviceIdType.MESH
VMEM_LIMIT = 60 * 1024 * 1024

mask_penalty = 1000000000.0
norm_epsilon = 1e-05


def normalize(values, gain):
    center = values - jnp.mean(values, axis=-1, keepdims=True)
    variance = jnp.mean(center * center, axis=-1, keepdims=True)
    return center * lax.rsqrt(variance + norm_epsilon) * gain


def mirror(tile):
    tile_rows, tile_cols, channels = tile.shape
    col_count = lax.axis_size("col")
    row_count = lax.axis_size("row")
    col_ratio = col_count // row_count
    piece_len = tile_cols * tile_cols // col_count
    sectioned = tile.reshape(col_ratio, col_count, piece_len, channels)
    sectioned = lax.all_to_all(sectioned, "col", split_axis=1, concat_axis=1, tiled=True)
    sectioned = sectioned.reshape(col_ratio, row_count, col_ratio, piece_len, channels)
    sectioned = lax.all_to_all(sectioned, "row", split_axis=1, concat_axis=1, tiled=True)
    sectioned = jnp.transpose(sectioned, (1, 0, 2, 3, 4)).reshape(
        col_count, col_ratio, piece_len, channels
    )
    sectioned = lax.all_to_all(sectioned, "col", split_axis=0, concat_axis=0, tiled=True)
    sectioned = jnp.transpose(sectioned, (1, 0, 2, 3)).reshape(
        col_ratio, tile_cols, tile_cols, channels
    )
    return jnp.transpose(sectioned, (0, 2, 1, 3)).reshape(tile_rows, tile_cols, channels)


def attend(query_part, gate_part, key_part, value_part, bias_part, head_count, output_weight):
    query_total = query_part.shape[0]
    key_total = key_part.shape[0]
    head_dim = query_part.shape[1] // head_count
    score_scale = 1.0 / math.sqrt(head_dim)
    query_heads = query_part.reshape(query_total, head_count, head_dim)
    key_heads = key_part.reshape(key_total, head_count, head_dim)
    value_heads = value_part.reshape(key_total, head_count, head_dim)
    scores = (
        jnp.einsum("jhd,khd->hjk", query_heads, key_heads, preferred_element_type=jnp.float32)
        * score_scale
        + bias_part
    )
    row_max = jnp.max(scores, axis=-1, keepdims=True)
    exponent = jnp.exp(scores - row_max)
    attn_weights = (exponent / jnp.sum(exponent, axis=-1, keepdims=True)).astype(jnp.bfloat16)
    mixture = jnp.einsum(
        "hjk,khd->jhd", attn_weights, value_heads, preferred_element_type=jnp.float32
    )
    gated = (gate_part * mixture.reshape(query_total, head_count * head_dim)).astype(jnp.bfloat16)
    return jnp.dot(gated, output_weight, preferred_element_type=jnp.float32).astype(jnp.bfloat16)


def mirror_layout(
    normed_tile,
    bias_tile,
    chain_ids,
    penalty,
    chain_weight,
    query_weight,
    key_weight,
    value_weight,
    gate_weight,
    output_weight,
):
    tile_rows, tile_cols, channels = normed_tile.shape
    head_count = bias_tile.shape[0]
    row_start = lax.axis_index("row") * tile_rows
    flat_tile = normed_tile.reshape(tile_rows * tile_cols, channels)
    key_tile = (
        jnp.dot(flat_tile, key_weight, preferred_element_type=jnp.float32)
        .astype(jnp.bfloat16)
        .reshape(tile_rows, tile_cols, -1)
    )
    value_tile = (
        jnp.dot(flat_tile, value_weight, preferred_element_type=jnp.float32)
        .astype(jnp.bfloat16)
        .reshape(tile_rows, tile_cols, -1)
    )
    key_all, value_all = (
        lax.all_gather(key_tile, "row", axis=0, tiled=True),
        lax.all_gather(value_tile, "row", axis=0, tiled=True),
    )
    bias_rows = lax.all_gather(bias_tile, "col", axis=2, tiled=True)
    chain_rows = lax.dynamic_slice_in_dim(chain_ids, row_start, tile_rows, 0)
    same_chain = (chain_rows[:, None] == chain_ids[None, :]).astype(jnp.float32)
    bias_full = (
        bias_rows.astype(jnp.float32)
        + chain_weight[:, None, None] * same_chain[None]
        - penalty[None, None, :]
    )
    query_tile = (
        jnp.dot(flat_tile, query_weight, preferred_element_type=jnp.float32)
        .astype(jnp.bfloat16)
        .reshape(tile_rows, tile_cols, -1)
    )
    gate_tile = jax.nn.sigmoid(
        jnp.dot(flat_tile, gate_weight, preferred_element_type=jnp.float32)
    ).reshape(tile_rows, tile_cols, -1)

    def one_column(position):
        query_part = lax.dynamic_index_in_dim(query_tile, position, 1, keepdims=False)
        gate_part = lax.dynamic_index_in_dim(gate_tile, position, 1, keepdims=False)
        key_part = lax.dynamic_index_in_dim(key_all, position, 1, keepdims=False)
        value_part = lax.dynamic_index_in_dim(value_all, position, 1, keepdims=False)
        return attend(
            query_part, gate_part, key_part, value_part, bias_full, head_count, output_weight
        )

    results = lax.map(one_column, jnp.arange(tile_cols, dtype=jnp.int32))
    return jnp.transpose(results, (1, 0, 2))


def tile_layout(
    pair_state,
    residue_mask,
    chain_ids,
    gain_transition,
    hidden_weight,
    out_weight,
    gain_attention,
    query_weight,
    key_weight,
    value_weight,
    gate_weight,
    bias_weight,
    chain_weight,
    output_weight,
):
    tile_rows, tile_cols, channels = pair_state.shape
    head_count = chain_weight.shape[0]
    mirrored = mirror(pair_state)
    sym_tile = pair_state.astype(jnp.float32) + mirrored.astype(jnp.float32)
    flat_sym = sym_tile.reshape(tile_rows * tile_cols, channels)
    first_norm = normalize(flat_sym, gain_transition).astype(jnp.bfloat16)
    hidden_act = jax.nn.relu(
        jnp.dot(first_norm, hidden_weight, preferred_element_type=jnp.float32)
    ).astype(jnp.bfloat16)
    carried = flat_sym + jnp.dot(hidden_act, out_weight, preferred_element_type=jnp.float32)
    normed = normalize(carried, gain_attention).astype(jnp.bfloat16)
    bias_tile = (
        jnp.einsum("pd,dh->hp", normed, bias_weight, preferred_element_type=jnp.float32)
        .astype(jnp.bfloat16)
        .reshape(head_count, tile_rows, tile_cols)
    )
    penalty = mask_penalty * (1 - residue_mask).astype(jnp.float32)
    normed_tile = normed.reshape(tile_rows, tile_cols, channels)
    arguments = (
        normed_tile,
        bias_tile,
        chain_ids,
        penalty,
        chain_weight,
        query_weight,
        key_weight,
        value_weight,
        gate_weight,
        output_weight,
    )
    own_update = mirror_layout(*arguments)
    other_update = mirror(own_update)
    total = (
        2.0 * carried.reshape(tile_rows, tile_cols, channels)
        + own_update.astype(jnp.float32)
        + other_update.astype(jnp.float32)
    )
    return total.astype(jnp.bfloat16)


def greet_all(row_count, col_count):
    device_total = row_count * col_count
    me = lax.axis_index("col") * row_count + lax.axis_index("row")
    barrier = pltpu.get_barrier_semaphore()

    def greet(step, carry):
        peer = lax.rem(me + step, device_total)
        pl.semaphore_signal(
            barrier,
            inc=1,
            device_id=(lax.rem(peer, row_count), peer // row_count),
            device_id_type=MESH,
        )
        return carry

    lax.fori_loop(1, device_total, greet, 0)
    pl.semaphore_wait(barrier, device_total - 1)


def transition_kernel(
    row_count,
    col_count,
    tile_ref,
    turned_ref,
    gain_transition_ref,
    hidden_weight_ref,
    out_weight_ref,
    gain_attention_ref,
    bias_weight_ref,
    carried_ref,
    normed_ref,
    bias_ref,
    row_buf,
    col_buf,
    relay_buf,
    relay_send,
    relay_recv,
    row_send,
    row_recv,
    col_send,
    col_recv,
    bias_send,
    bias_recv,
    pair_send,
    pair_recv,
):
    tile_rows, tile_cols, channels = tile_ref.shape
    own = tile_cols // row_count
    span = col_count // row_count
    chip_total = row_count * col_count // 2
    row_id, col_id = lax.axis_index("row"), lax.axis_index("col")
    me = col_id * row_count + row_id
    side = lax.rem(col_id, 2)
    chip = (col_id // 2) * row_count + row_id
    greet_all(row_count, col_count)

    def relay_copy(other, slot):
        return pltpu.make_async_remote_copy(
            src_ref=tile_ref.at[pl.ds((slot * row_count + other) * own, own)],
            dst_ref=relay_buf.at[row_id, slot],
            send_sem=relay_send.at[other, slot],
            recv_sem=relay_recv.at[row_id, slot],
            device_id=(other, col_id),
            device_id_type=MESH,
        )

    def start_rows(origin, slot, source):
        target = origin * span + slot
        landing = row_buf.at[:, pl.ds(pl.multiple_of(col_id * tile_cols, tile_cols), tile_cols), :]

        @pl.when(target != col_id)
        def _():
            pltpu.make_async_remote_copy(
                src_ref=source,
                dst_ref=landing,
                send_sem=row_send.at[origin, slot],
                recv_sem=row_recv.at[col_id],
                device_id=(row_id, target),
                device_id_type=MESH,
            ).start()

        @pl.when(target == col_id)
        def _():
            pltpu.make_async_copy(source, landing, row_recv.at[col_id]).start()

    def col_remote(other):
        return pltpu.make_async_remote_copy(
            src_ref=turned_ref.at[pl.ds(other * own, own)],
            dst_ref=col_buf.at[
                :, pl.ds(pl.multiple_of(row_id * tile_rows, tile_rows), tile_rows), :
            ],
            send_sem=col_send.at[other],
            recv_sem=col_recv.at[row_id],
            device_id=(other, col_id),
            device_id_type=MESH,
        )

    def over_rows(body):
        def one(step, carry):
            body(lax.rem(row_id + step, row_count))
            return carry

        lax.fori_loop(1, row_count, one, 0)

    def over_slots(body):
        def one(step, carry):
            body(lax.rem(col_id + step, span))
            return carry

        lax.fori_loop(0, span, one, 0)

    over_rows(lambda other: over_slots(lambda slot: relay_copy(other, slot).start()))
    over_slots(
        lambda slot: start_rows(
            row_id, slot, tile_ref.at[pl.ds((slot * row_count + row_id) * own, own)]
        )
    )
    over_rows(lambda other: col_remote(other).start())
    own_col = pltpu.make_async_copy(
        turned_ref.at[pl.ds(row_id * own, own)],
        col_buf.at[:, pl.ds(pl.multiple_of(row_id * tile_rows, tile_rows), tile_rows), :],
        col_recv.at[row_id],
    )
    own_col.start()

    def pass_on(origin, slot):
        arrived = relay_buf.at[origin, slot]
        pltpu.make_async_copy(arrived, arrived, relay_recv.at[origin, slot]).wait()
        start_rows(origin, slot, arrived)

    over_rows(lambda origin: over_slots(lambda slot: pass_on(origin, slot)))

    def wait_row(other, carry):
        landed = row_buf.at[:, pl.ds(pl.multiple_of(other * tile_cols, tile_cols), tile_cols), :]
        pltpu.make_async_copy(landed, landed, row_recv.at[other]).wait()
        return carry

    lax.fori_loop(0, col_count, wait_row, 0)

    def wait_col(other, carry):
        landed = col_buf.at[:, pl.ds(pl.multiple_of(other * tile_rows, tile_rows), tile_rows), :]
        pltpu.make_async_copy(landed, landed, col_recv.at[other]).wait()
        return carry

    lax.fori_loop(0, row_count, wait_col, 0)

    def over_chips(body):
        def one(step, carry):
            body(lax.rem(chip + step, chip_total))
            return carry

        lax.fori_loop(1, chip_total, one, 0)

    def chip_place(other, which):
        return lax.rem(other, row_count), (other // row_count) * 2 + which

    def slab(other, which):
        place = chip_place(other, which)
        return bias_ref.at[pl.ds((place[1] * row_count + place[0]) * own, own)]

    def one_row(position, carry):
        sym_row = row_buf[position].astype(jnp.float32) + col_buf[position].astype(jnp.float32)
        first_norm = normalize(sym_row, gain_transition_ref[...]).astype(jnp.bfloat16)
        hidden_act = jax.nn.relu(
            jnp.dot(first_norm, hidden_weight_ref[...], preferred_element_type=jnp.float32)
        ).astype(jnp.bfloat16)
        carried = sym_row + jnp.dot(
            hidden_act, out_weight_ref[...], preferred_element_type=jnp.float32
        )
        carried_ref[position] = carried
        normed = normalize(carried, gain_attention_ref[...]).astype(jnp.bfloat16)
        normed_ref[position] = normed
        bias_ref[me * own + position] = lax.dot_general(
            bias_weight_ref[...],
            normed,
            (((1,), (1,)), ((), ())),
            preferred_element_type=jnp.float32,
        ).astype(jnp.bfloat16)
        over_chips(
            lambda other: pltpu.make_async_remote_copy(
                src_ref=bias_ref.at[me * own + position],
                dst_ref=bias_ref.at[me * own + position],
                send_sem=bias_send.at[other],
                recv_sem=bias_recv.at[chip],
                device_id=chip_place(other, side),
                device_id_type=MESH,
            ).start()
        )
        return carry

    lax.fori_loop(0, own, one_row, 0)

    def to_pair(other):
        return pltpu.make_async_remote_copy(
            src_ref=slab(other, side),
            dst_ref=slab(other, side),
            send_sem=pair_send.at[other],
            recv_sem=pair_recv.at[other],
            device_id=(row_id, col_id + 1 - 2 * side),
            device_id_type=MESH,
        )

    to_pair(chip).start()

    def hand_over(other):
        landed = slab(other, side)
        pltpu.make_async_copy(landed, landed, bias_recv.at[other]).wait()
        to_pair(other).start()

    over_chips(hand_over)

    def close_pair(other, carry):
        landed = slab(other, 1 - side)
        pltpu.make_async_copy(landed, landed, pair_recv.at[other]).wait()
        to_pair(other).wait_send()
        return carry

    lax.fori_loop(0, chip_total, close_pair, 0)

    def close_chip(other):
        sent = slab(chip, side)
        pltpu.make_async_copy(sent, sent, bias_send.at[other]).wait()

    over_chips(close_chip)

    def close_rows(origin, slot):
        @pl.when(origin * span + slot != col_id)
        def _():
            sent = relay_buf.at[origin, slot]
            pltpu.make_async_copy(sent, sent, row_send.at[origin, slot]).wait()

    over_slots(lambda slot: close_rows(row_id, slot))
    over_rows(lambda origin: over_slots(lambda slot: close_rows(origin, slot)))
    over_rows(lambda other: over_slots(lambda slot: relay_copy(other, slot).wait_send()))
    over_rows(lambda other: col_remote(other).wait_send())


def attention_kernel(
    row_count,
    col_count,
    carried_ref,
    normed_ref,
    bias_ref,
    query_weight_ref,
    key_weight_ref,
    value_weight_ref,
    gate_weight_ref,
    output_weight_ref,
    out_ref,
    total,
    update_buf,
    recv_buf,
    turned,
    sum_buf,
    update_send,
    update_recv,
    sum_send,
    sum_recv,
):
    own, length, channels = normed_ref.shape
    head_count = bias_ref.shape[0]
    head_dim = query_weight_ref.shape[1] // head_count
    score_scale = 1.0 / math.sqrt(head_dim)
    tile_rows = length // row_count
    device_total = row_count * col_count
    row_id, col_id = lax.axis_index("row"), lax.axis_index("col")
    me = col_id * row_count + row_id
    greet_all(row_count, col_count)

    def update_remote(position, peer):
        return pltpu.make_async_remote_copy(
            src_ref=update_buf.at[position, peer],
            dst_ref=recv_buf.at[me * own + position],
            send_sem=update_send.at[peer],
            recv_sem=update_recv.at[me],
            device_id=(lax.rem(peer, row_count), peer // row_count),
            device_id_type=MESH,
        )

    head_of_lane = lax.broadcasted_iota(jnp.int32, (1, channels), 1) // head_dim

    def one_row(position, carry):
        normed = normed_ref[position]

        def project(weight_ref):
            return jnp.dot(normed, weight_ref[...], preferred_element_type=jnp.float32)

        queries = project(query_weight_ref).astype(jnp.bfloat16)
        keys_turned = project(key_weight_ref).astype(jnp.bfloat16).T
        values = project(value_weight_ref).astype(jnp.bfloat16)
        gates = jax.nn.sigmoid(project(gate_weight_ref))
        mixture = jnp.zeros((length, channels), jnp.float32)
        for head in range(head_count):
            chosen = (head_of_lane == head).astype(jnp.bfloat16)
            scores = (
                jnp.dot(queries * chosen, keys_turned, preferred_element_type=jnp.float32)
                * score_scale
                + bias_ref[head]
            )
            row_max = jnp.max(scores, axis=-1, keepdims=True)
            exponent = jnp.exp(scores - row_max)
            attn_weights = (
                exponent * (1.0 / jnp.sum(exponent, axis=-1, keepdims=True))
            ).astype(jnp.bfloat16)
            mixture = mixture + jnp.dot(
                attn_weights, values * chosen, preferred_element_type=jnp.float32
            )
        gated = (gates * mixture).astype(jnp.bfloat16)
        update = jnp.dot(gated, output_weight_ref[...], preferred_element_type=jnp.float32)
        update = update.reshape(device_total, own, channels).astype(jnp.bfloat16)
        update_buf[position] = update
        recv_buf[me * own + position] = update_buf[position, me]
        total[position] = 2.0 * carried_ref[position] + update.astype(jnp.float32).reshape(
            length, channels
        )

        def send(step, inner):
            update_remote(position, lax.rem(me + step, device_total)).start()
            return inner

        lax.fori_loop(1, device_total, send, 0)
        return carry

    lax.fori_loop(0, own, one_row, 0)
    for position in range(own):
        turned[:, position, :] = total[position]

    def wait_update(step, carry):
        peer = lax.rem(me + step, device_total)
        landed = recv_buf.at[pl.ds(peer * own, own)]
        pltpu.make_async_copy(landed, landed, update_recv.at[peer]).wait()
        pltpu.make_async_copy(landed, landed, update_send.at[peer]).wait()
        return carry

    lax.fori_loop(1, device_total, wait_update, 0)

    def sum_remote(other):
        return pltpu.make_async_remote_copy(
            src_ref=sum_buf.at[other],
            dst_ref=out_ref.at[row_id],
            send_sem=sum_send.at[other],
            recv_sem=sum_recv.at[row_id],
            device_id=(other, col_id),
            device_id_type=MESH,
        )

    def sum_rows(other, target_ref):
        def one_block(block, carry):
            rows = pl.ds(other * tile_rows + block * own, own)
            summed = turned[rows] + recv_buf[rows].astype(jnp.float32)
            target_ref[other, pl.ds(block * own, own)] = summed.astype(jnp.bfloat16)
            return carry

        lax.fori_loop(0, tile_rows // own, one_block, 0)

    def send_sum(step, carry):
        other = lax.rem(row_id + step, row_count)
        sum_rows(other, sum_buf)
        sum_remote(other).start()
        return carry

    lax.fori_loop(1, row_count, send_sum, 0)
    sum_rows(row_id, out_ref)

    def wait_sum(step, carry):
        other = lax.rem(row_id + step, row_count)
        landed = out_ref.at[other]
        pltpu.make_async_copy(landed, landed, sum_recv.at[other]).wait()
        sum_remote(other).wait_send()
        return carry

    lax.fori_loop(1, row_count, wait_sum, 0)


def owned_columns(
    pair_state,
    residue_mask,
    chain_ids,
    gain_transition,
    hidden_weight,
    out_weight,
    gain_attention,
    query_weight,
    key_weight,
    value_weight,
    gate_weight,
    bias_weight,
    chain_weight,
    output_weight,
):
    tile_rows, tile_cols, channels = pair_state.shape
    row_count, col_count = lax.axis_size("row"), lax.axis_size("col")
    device_total = row_count * col_count
    head_count = chain_weight.shape[0]
    length = tile_rows * row_count
    own = tile_cols // row_count
    span = col_count // row_count
    in_vmem = pl.BlockSpec(memory_space=pltpu.VMEM)
    dma = pltpu.SemaphoreType.DMA
    carried, normed, bias_rows = pl.pallas_call(
        functools.partial(transition_kernel, row_count, col_count),
        out_shape=(
            jax.ShapeDtypeStruct((own, length, channels), jnp.float32),
            jax.ShapeDtypeStruct((own, length, channels), jnp.bfloat16),
            jax.ShapeDtypeStruct((length, head_count, length), jnp.bfloat16),
        ),
        in_specs=[in_vmem] * 7,
        out_specs=(in_vmem,) * 3,
        scratch_shapes=[
            pltpu.VMEM((own, length, channels), jnp.bfloat16),
            pltpu.VMEM((own, length, channels), jnp.bfloat16),
            pltpu.VMEM((row_count, span, own, tile_cols, channels), jnp.bfloat16),
            dma((row_count, span)),
            dma((row_count, span)),
            dma((row_count, span)),
            dma((col_count,)),
            dma((row_count,)),
            dma((row_count,)),
            dma((device_total // 2,)),
            dma((device_total // 2,)),
            dma((device_total // 2,)),
            dma((device_total // 2,)),
        ],
        compiler_params=pltpu.CompilerParams(
            collective_id=0, has_side_effects=True, vmem_limit_bytes=VMEM_LIMIT
        ),
        name="transition",
    )(
        pair_state,
        jnp.transpose(pair_state, (1, 0, 2)),
        gain_transition[None, :],
        hidden_weight,
        out_weight,
        gain_attention[None, :],
        bias_weight.T,
    )
    penalty = mask_penalty * (1 - residue_mask).astype(jnp.float32)
    same_chain = (chain_ids[:, None] == chain_ids[None, :]).astype(jnp.float32)
    bias_full = (
        jnp.transpose(bias_rows, (1, 0, 2)).astype(jnp.float32)
        + chain_weight[:, None, None] * same_chain[None]
        - penalty[None, None, :]
    )
    pieces = pl.pallas_call(
        functools.partial(attention_kernel, row_count, col_count),
        out_shape=jax.ShapeDtypeStruct((row_count, tile_rows, own, channels), jnp.bfloat16),
        in_specs=[in_vmem] * 8,
        out_specs=in_vmem,
        scratch_shapes=[
            pltpu.VMEM((own, length, channels), jnp.float32),
            pltpu.VMEM((own, device_total, own, channels), jnp.bfloat16),
            pltpu.VMEM((length, own, channels), jnp.bfloat16),
            pltpu.VMEM((length, own, channels), jnp.float32),
            pltpu.VMEM((row_count, tile_rows, own, channels), jnp.bfloat16),
            dma((device_total,)),
            dma((device_total,)),
            dma((row_count,)),
            dma((row_count,)),
        ],
        compiler_params=pltpu.CompilerParams(
            collective_id=1, has_side_effects=True, vmem_limit_bytes=VMEM_LIMIT
        ),
        name="attention",
    )(
        carried,
        normed,
        bias_full,
        query_weight,
        key_weight,
        value_weight,
        gate_weight,
        output_weight,
    )
    return jnp.transpose(pieces, (1, 0, 2, 3)).reshape(tile_rows, tile_cols, channels)


def per_device(pair_state, *others):
    tile_cols = pair_state.shape[1]
    row_count, col_count = lax.axis_size("row"), lax.axis_size("col")
    own = tile_cols // row_count
    if own % 8 == 0 and col_count % 2 == 0 and col_count % row_count == 0:
        return owned_columns(pair_state, *others)
    return tile_layout(pair_state, *others)


def solution(mesh):
    placed = (
        P("row", "col", None),
        P(),
        P(),
        P(),
        P(),
        P(),
        P(),
        P(),
        P(),
        P(),
        P(),
        P(),
        P(),
        P(),
    )
    return jax.shard_map(
        per_device, mesh=mesh, in_specs=placed, out_specs=P("row", "col", None), check_vma=False
    )
```

```python
import functools
import math

import jax
import jax.numpy as jnp
from jax import lax
from jax.experimental import pallas as pl
from jax.experimental.pallas import tpu as pltpu
from jax.sharding import PartitionSpec as P

MESH = pl.DeviceIdType.MESH
VMEM_LIMIT = 60 * 1024 * 1024
LOG2_E = math.log2(math.e)

mask_penalty = 1000000000.0
norm_epsilon = 1e-05


def normalize(values, gain):
    center = values - jnp.mean(values, axis=-1, keepdims=True)
    variance = jnp.mean(center * center, axis=-1, keepdims=True)
    return center * lax.rsqrt(variance + norm_epsilon) * gain


def mirror(tile):
    tile_rows, tile_cols, channels = tile.shape
    col_count = lax.axis_size("col")
    row_count = lax.axis_size("row")
    col_ratio = col_count // row_count
    piece_len = tile_cols * tile_cols // col_count
    sectioned = tile.reshape(col_ratio, col_count, piece_len, channels)
    sectioned = lax.all_to_all(sectioned, "col", split_axis=1, concat_axis=1, tiled=True)
    sectioned = sectioned.reshape(col_ratio, row_count, col_ratio, piece_len, channels)
    sectioned = lax.all_to_all(sectioned, "row", split_axis=1, concat_axis=1, tiled=True)
    sectioned = jnp.transpose(sectioned, (1, 0, 2, 3, 4)).reshape(
        col_count, col_ratio, piece_len, channels
    )
    sectioned = lax.all_to_all(sectioned, "col", split_axis=0, concat_axis=0, tiled=True)
    sectioned = jnp.transpose(sectioned, (1, 0, 2, 3)).reshape(
        col_ratio, tile_cols, tile_cols, channels
    )
    return jnp.transpose(sectioned, (0, 2, 1, 3)).reshape(tile_rows, tile_cols, channels)


def attend(query_part, gate_part, key_part, value_part, bias_part, head_count, output_weight):
    query_total = query_part.shape[0]
    key_total = key_part.shape[0]
    head_dim = query_part.shape[1] // head_count
    score_scale = 1.0 / math.sqrt(head_dim)
    query_heads = query_part.reshape(query_total, head_count, head_dim)
    key_heads = key_part.reshape(key_total, head_count, head_dim)
    value_heads = value_part.reshape(key_total, head_count, head_dim)
    scores = (
        jnp.einsum("jhd,khd->hjk", query_heads, key_heads, preferred_element_type=jnp.float32)
        * score_scale
        + bias_part
    )
    row_max = jnp.max(scores, axis=-1, keepdims=True)
    exponent = jnp.exp(scores - row_max)
    attn_weights = (exponent / jnp.sum(exponent, axis=-1, keepdims=True)).astype(jnp.bfloat16)
    mixture = jnp.einsum(
        "hjk,khd->jhd", attn_weights, value_heads, preferred_element_type=jnp.float32
    )
    gated = (gate_part * mixture.reshape(query_total, head_count * head_dim)).astype(jnp.bfloat16)
    return jnp.dot(gated, output_weight, preferred_element_type=jnp.float32).astype(jnp.bfloat16)


def mirror_layout(
    normed_tile,
    bias_tile,
    chain_ids,
    penalty,
    chain_weight,
    query_weight,
    key_weight,
    value_weight,
    gate_weight,
    output_weight,
):
    tile_rows, tile_cols, channels = normed_tile.shape
    head_count = bias_tile.shape[0]
    row_start = lax.axis_index("row") * tile_rows
    flat_tile = normed_tile.reshape(tile_rows * tile_cols, channels)
    key_tile = (
        jnp.dot(flat_tile, key_weight, preferred_element_type=jnp.float32)
        .astype(jnp.bfloat16)
        .reshape(tile_rows, tile_cols, -1)
    )
    value_tile = (
        jnp.dot(flat_tile, value_weight, preferred_element_type=jnp.float32)
        .astype(jnp.bfloat16)
        .reshape(tile_rows, tile_cols, -1)
    )
    key_all, value_all = (
        lax.all_gather(key_tile, "row", axis=0, tiled=True),
        lax.all_gather(value_tile, "row", axis=0, tiled=True),
    )
    bias_rows = lax.all_gather(bias_tile, "col", axis=2, tiled=True)
    chain_rows = lax.dynamic_slice_in_dim(chain_ids, row_start, tile_rows, 0)
    same_chain = (chain_rows[:, None] == chain_ids[None, :]).astype(jnp.float32)
    bias_full = (
        bias_rows.astype(jnp.float32)
        + chain_weight[:, None, None] * same_chain[None]
        - penalty[None, None, :]
    )
    query_tile = (
        jnp.dot(flat_tile, query_weight, preferred_element_type=jnp.float32)
        .astype(jnp.bfloat16)
        .reshape(tile_rows, tile_cols, -1)
    )
    gate_tile = jax.nn.sigmoid(
        jnp.dot(flat_tile, gate_weight, preferred_element_type=jnp.float32)
    ).reshape(tile_rows, tile_cols, -1)

    def one_column(position):
        query_part = lax.dynamic_index_in_dim(query_tile, position, 1, keepdims=False)
        gate_part = lax.dynamic_index_in_dim(gate_tile, position, 1, keepdims=False)
        key_part = lax.dynamic_index_in_dim(key_all, position, 1, keepdims=False)
        value_part = lax.dynamic_index_in_dim(value_all, position, 1, keepdims=False)
        return attend(
            query_part, gate_part, key_part, value_part, bias_full, head_count, output_weight
        )

    results = lax.map(one_column, jnp.arange(tile_cols, dtype=jnp.int32))
    return jnp.transpose(results, (1, 0, 2))


def tile_layout(
    pair_state,
    residue_mask,
    chain_ids,
    gain_transition,
    hidden_weight,
    out_weight,
    gain_attention,
    query_weight,
    key_weight,
    value_weight,
    gate_weight,
    bias_weight,
    chain_weight,
    output_weight,
):
    tile_rows, tile_cols, channels = pair_state.shape
    head_count = chain_weight.shape[0]
    mirrored = mirror(pair_state)
    sym_tile = pair_state.astype(jnp.float32) + mirrored.astype(jnp.float32)
    flat_sym = sym_tile.reshape(tile_rows * tile_cols, channels)
    first_norm = normalize(flat_sym, gain_transition).astype(jnp.bfloat16)
    hidden_act = jax.nn.relu(
        jnp.dot(first_norm, hidden_weight, preferred_element_type=jnp.float32)
    ).astype(jnp.bfloat16)
    carried = flat_sym + jnp.dot(hidden_act, out_weight, preferred_element_type=jnp.float32)
    normed = normalize(carried, gain_attention).astype(jnp.bfloat16)
    bias_tile = (
        jnp.einsum("pd,dh->hp", normed, bias_weight, preferred_element_type=jnp.float32)
        .astype(jnp.bfloat16)
        .reshape(head_count, tile_rows, tile_cols)
    )
    penalty = mask_penalty * (1 - residue_mask).astype(jnp.float32)
    normed_tile = normed.reshape(tile_rows, tile_cols, channels)
    arguments = (
        normed_tile,
        bias_tile,
        chain_ids,
        penalty,
        chain_weight,
        query_weight,
        key_weight,
        value_weight,
        gate_weight,
        output_weight,
    )
    own_update = mirror_layout(*arguments)
    other_update = mirror(own_update)
    total = (
        2.0 * carried.reshape(tile_rows, tile_cols, channels)
        + own_update.astype(jnp.float32)
        + other_update.astype(jnp.float32)
    )
    return total.astype(jnp.bfloat16)


def greet_all(row_count, col_count):
    device_total = row_count * col_count
    me = lax.axis_index("col") * row_count + lax.axis_index("row")
    barrier = pltpu.get_barrier_semaphore()

    def greet(step, carry):
        peer = lax.rem(me + step, device_total)
        pl.semaphore_signal(
            barrier,
            inc=1,
            device_id=(lax.rem(peer, row_count), peer // row_count),
            device_id_type=MESH,
        )
        return carry

    lax.fori_loop(1, device_total, greet, 0)
    pl.semaphore_wait(barrier, device_total - 1)


def transition_kernel(
    row_count,
    col_count,
    tile_ref,
    turned_ref,
    gain_transition_ref,
    hidden_weight_ref,
    out_weight_ref,
    gain_attention_ref,
    bias_weight_ref,
    carried_ref,
    normed_ref,
    bias_ref,
    row_buf,
    col_buf,
    relay_buf,
    relay_send,
    relay_recv,
    row_send,
    row_recv,
    col_send,
    col_recv,
    bias_send,
    bias_recv,
    pair_send,
    pair_recv,
):
    tile_rows, tile_cols, channels = tile_ref.shape
    own = tile_cols // row_count
    span = col_count // row_count
    chip_total = row_count * col_count // 2
    row_id, col_id = lax.axis_index("row"), lax.axis_index("col")
    me = col_id * row_count + row_id
    side = lax.rem(col_id, 2)
    chip = (col_id // 2) * row_count + row_id
    greet_all(row_count, col_count)

    def relay_copy(other, slot):
        return pltpu.make_async_remote_copy(
            src_ref=tile_ref.at[pl.ds((slot * row_count + other) * own, own)],
            dst_ref=relay_buf.at[row_id, slot],
            send_sem=relay_send.at[other, slot],
            recv_sem=relay_recv.at[row_id, slot],
            device_id=(other, col_id),
            device_id_type=MESH,
        )

    def start_rows(origin, slot, source):
        target = origin * span + slot
        landing = row_buf.at[:, pl.ds(pl.multiple_of(col_id * tile_cols, tile_cols), tile_cols), :]

        @pl.when(target != col_id)
        def _():
            pltpu.make_async_remote_copy(
                src_ref=source,
                dst_ref=landing,
                send_sem=row_send.at[origin, slot],
                recv_sem=row_recv.at[col_id],
                device_id=(row_id, target),
                device_id_type=MESH,
            ).start()

        @pl.when(target == col_id)
        def _():
            pltpu.make_async_copy(source, landing, row_recv.at[col_id]).start()

    def col_remote(other):
        return pltpu.make_async_remote_copy(
            src_ref=turned_ref.at[pl.ds(other * own, own)],
            dst_ref=col_buf.at[
                :, pl.ds(pl.multiple_of(row_id * tile_rows, tile_rows), tile_rows), :
            ],
            send_sem=col_send.at[other],
            recv_sem=col_recv.at[row_id],
            device_id=(other, col_id),
            device_id_type=MESH,
        )

    def over_rows(body):
        def one(step, carry):
            body(lax.rem(row_id + step, row_count))
            return carry

        lax.fori_loop(1, row_count, one, 0)

    def over_slots(body):
        def one(step, carry):
            body(lax.rem(col_id + step, span))
            return carry

        lax.fori_loop(0, span, one, 0)

    over_rows(lambda other: over_slots(lambda slot: relay_copy(other, slot).start()))
    over_slots(
        lambda slot: start_rows(
            row_id, slot, tile_ref.at[pl.ds((slot * row_count + row_id) * own, own)]
        )
    )
    over_rows(lambda other: col_remote(other).start())
    own_col = pltpu.make_async_copy(
        turned_ref.at[pl.ds(row_id * own, own)],
        col_buf.at[:, pl.ds(pl.multiple_of(row_id * tile_rows, tile_rows), tile_rows), :],
        col_recv.at[row_id],
    )
    own_col.start()

    def pass_on(origin, slot):
        arrived = relay_buf.at[origin, slot]
        pltpu.make_async_copy(arrived, arrived, relay_recv.at[origin, slot]).wait()
        start_rows(origin, slot, arrived)

    over_rows(lambda origin: over_slots(lambda slot: pass_on(origin, slot)))

    def wait_row(other, carry):
        landed = row_buf.at[:, pl.ds(pl.multiple_of(other * tile_cols, tile_cols), tile_cols), :]
        pltpu.make_async_copy(landed, landed, row_recv.at[other]).wait()
        return carry

    lax.fori_loop(0, col_count, wait_row, 0)

    def wait_col(other, carry):
        landed = col_buf.at[:, pl.ds(pl.multiple_of(other * tile_rows, tile_rows), tile_rows), :]
        pltpu.make_async_copy(landed, landed, col_recv.at[other]).wait()
        return carry

    lax.fori_loop(0, row_count, wait_col, 0)

    def over_chips(body):
        def one(step, carry):
            body(lax.rem(chip + step, chip_total))
            return carry

        lax.fori_loop(1, chip_total, one, 0)

    def chip_place(other, which):
        return lax.rem(other, row_count), (other // row_count) * 2 + which

    def slab(other, which):
        place = chip_place(other, which)
        return bias_ref.at[pl.ds((place[1] * row_count + place[0]) * own, own)]

    def one_row(position, carry):
        sym_row = row_buf[position].astype(jnp.float32) + col_buf[position].astype(jnp.float32)
        first_norm = normalize(sym_row, gain_transition_ref[...]).astype(jnp.bfloat16)
        hidden_act = jax.nn.relu(
            jnp.dot(first_norm, hidden_weight_ref[...], preferred_element_type=jnp.float32)
        ).astype(jnp.bfloat16)
        carried = sym_row + jnp.dot(
            hidden_act, out_weight_ref[...], preferred_element_type=jnp.float32
        )
        carried_ref[position] = carried
        normed = normalize(carried, gain_attention_ref[...]).astype(jnp.bfloat16)
        normed_ref[position] = normed
        bias_ref[me * own + position] = lax.dot_general(
            bias_weight_ref[...],
            normed,
            (((1,), (1,)), ((), ())),
            preferred_element_type=jnp.float32,
        ).astype(jnp.bfloat16)
        over_chips(
            lambda other: pltpu.make_async_remote_copy(
                src_ref=bias_ref.at[me * own + position],
                dst_ref=bias_ref.at[me * own + position],
                send_sem=bias_send.at[other],
                recv_sem=bias_recv.at[chip],
                device_id=chip_place(other, side),
                device_id_type=MESH,
            ).start()
        )
        return carry

    lax.fori_loop(0, own, one_row, 0)

    def to_pair(other):
        return pltpu.make_async_remote_copy(
            src_ref=slab(other, side),
            dst_ref=slab(other, side),
            send_sem=pair_send.at[other],
            recv_sem=pair_recv.at[other],
            device_id=(row_id, col_id + 1 - 2 * side),
            device_id_type=MESH,
        )

    to_pair(chip).start()

    def hand_over(other):
        landed = slab(other, side)
        pltpu.make_async_copy(landed, landed, bias_recv.at[other]).wait()
        to_pair(other).start()

    over_chips(hand_over)

    def close_pair(other, carry):
        landed = slab(other, 1 - side)
        pltpu.make_async_copy(landed, landed, pair_recv.at[other]).wait()
        to_pair(other).wait_send()
        return carry

    lax.fori_loop(0, chip_total, close_pair, 0)

    def close_chip(other):
        sent = slab(chip, side)
        pltpu.make_async_copy(sent, sent, bias_send.at[other]).wait()

    over_chips(close_chip)

    def close_rows(origin, slot):
        @pl.when(origin * span + slot != col_id)
        def _():
            sent = relay_buf.at[origin, slot]
            pltpu.make_async_copy(sent, sent, row_send.at[origin, slot]).wait()

    over_slots(lambda slot: close_rows(row_id, slot))
    over_rows(lambda origin: over_slots(lambda slot: close_rows(origin, slot)))
    over_rows(lambda other: over_slots(lambda slot: relay_copy(other, slot).wait_send()))
    over_rows(lambda other: col_remote(other).wait_send())


def attention_kernel(
    row_count,
    col_count,
    carried_ref,
    normed_ref,
    bias_ref,
    query_turned_ref,
    key_weight_ref,
    value_turned_ref,
    gate_turned_ref,
    output_weight_ref,
    out_ref,
    total,
    update_buf,
    recv_buf,
    turned,
    sum_buf,
    update_send,
    update_recv,
    sum_send,
    sum_recv,
):
    own, length, channels = normed_ref.shape
    head_count = bias_ref.shape[0]
    inner_total = key_weight_ref.shape[1]
    head_dim = inner_total // head_count
    score_scale = LOG2_E / math.sqrt(head_dim)
    device_total = row_count * col_count
    row_id, col_id = lax.axis_index("row"), lax.axis_index("col")
    me = col_id * row_count + row_id
    greet_all(row_count, col_count)

    def over_peers(body):
        def one(step, carry):
            body(lax.rem(me + step, device_total))
            return carry

        lax.fori_loop(1, device_total, one, 0)

    def over_rows(body):
        def one(step, carry):
            body(lax.rem(row_id + step, row_count))
            return carry

        lax.fori_loop(1, row_count, one, 0)

    band = min(inner_total, max(128, head_dim))
    heads_in_band = band // head_dim
    head_of_lane = lax.broadcasted_iota(jnp.int32, (1, band), 1) // head_dim

    def one_row(position, carry):
        normed = normed_ref[position]
        normed_turned = normed.T

        def project(weight_ref):
            return jnp.dot(weight_ref[...], normed_turned, preferred_element_type=jnp.float32)

        keys = jnp.dot(
            normed, key_weight_ref[...], preferred_element_type=jnp.float32
        ).astype(jnp.bfloat16)
        queries = project(query_turned_ref).astype(jnp.bfloat16)
        values = project(value_turned_ref).astype(jnp.bfloat16)
        gates = jax.nn.sigmoid(project(gate_turned_ref))
        mixed = []
        for head in range(head_count):
            first = head // heads_in_band * band
            chosen = (head_of_lane == head % heads_in_band).astype(jnp.bfloat16)
            rows = slice(head * head_dim, (head + 1) * head_dim)
            scores = (
                jnp.dot(
                    keys[:, first : first + band] * chosen,
                    queries[first : first + band],
                    preferred_element_type=jnp.float32,
                )
                * score_scale
                + bias_ref[head]
            )
            exponent = jnp.exp2(scores - jnp.max(scores, axis=0, keepdims=True))
            attn_weights = (
                exponent * (1.0 / jnp.sum(exponent, axis=0, keepdims=True))
            ).astype(jnp.bfloat16)
            mixture = jnp.dot(values[rows], attn_weights, preferred_element_type=jnp.float32)
            mixed.append((gates[rows] * mixture).astype(jnp.bfloat16))
        gated = jnp.concatenate(mixed, axis=0).T
        update = jnp.dot(gated, output_weight_ref[...], preferred_element_type=jnp.float32)
        update = update.reshape(device_total, own, channels).astype(jnp.bfloat16)
        update_buf[position] = update
        recv_buf[me, position] = update_buf[position, me]
        total[position] = 2.0 * carried_ref[position] + update.astype(jnp.float32).reshape(
            length, channels
        )
        over_peers(
            lambda peer: pltpu.make_async_remote_copy(
                src_ref=update_buf.at[position, peer],
                dst_ref=recv_buf.at[me, position],
                send_sem=update_send.at[peer],
                recv_sem=update_recv.at[position, me],
                device_id=(lax.rem(peer, row_count), peer // row_count),
                device_id_type=MESH,
            ).start()
        )
        return carry

    lax.fori_loop(0, own, one_row, 0)
    for position in range(own):
        turned[:, :, position, :] = total[position].reshape(device_total, own, channels)

    def summed(other, position):
        devices = pl.ds(other * col_count, col_count)
        return (
            turned[devices, position] + recv_buf[devices, position].astype(jnp.float32)
        ).astype(jnp.bfloat16)

    def sum_remote(other, position):
        return pltpu.make_async_remote_copy(
            src_ref=sum_buf.at[other, :, position],
            dst_ref=out_ref.at[row_id, :, position],
            send_sem=sum_send.at[other, position],
            recv_sem=sum_recv.at[row_id, position],
            device_id=(other, col_id),
            device_id_type=MESH,
        )

    def finish_position(position, carry):
        def arrived(peer):
            landed = recv_buf.at[peer, position]
            pltpu.make_async_copy(landed, landed, update_recv.at[position, peer]).wait()

        over_peers(arrived)

        def pass_sum(other):
            sum_buf[other, :, position] = summed(other, position)
            sum_remote(other, position).start()

        over_rows(pass_sum)
        out_ref[row_id, :, position] = summed(row_id, position)
        return carry

    lax.fori_loop(0, own, finish_position, 0)

    def close_peer(peer):
        sent = recv_buf.at[peer]
        pltpu.make_async_copy(sent, sent, update_send.at[peer]).wait()

    over_peers(close_peer)

    def close_position(position, carry):
        def close_row(other):
            landed = out_ref.at[other, :, position]
            pltpu.make_async_copy(landed, landed, sum_recv.at[other, position]).wait()
            sum_remote(other, position).wait_send()

        over_rows(close_row)
        return carry

    lax.fori_loop(0, own, close_position, 0)


def owned_columns(
    pair_state,
    residue_mask,
    chain_ids,
    gain_transition,
    hidden_weight,
    out_weight,
    gain_attention,
    query_weight,
    key_weight,
    value_weight,
    gate_weight,
    bias_weight,
    chain_weight,
    output_weight,
):
    tile_rows, tile_cols, channels = pair_state.shape
    row_count, col_count = lax.axis_size("row"), lax.axis_size("col")
    device_total = row_count * col_count
    head_count = chain_weight.shape[0]
    length = tile_rows * row_count
    own = tile_cols // row_count
    span = col_count // row_count
    in_vmem = pl.BlockSpec(memory_space=pltpu.VMEM)
    dma = pltpu.SemaphoreType.DMA
    carried, normed, bias_rows = pl.pallas_call(
        functools.partial(transition_kernel, row_count, col_count),
        out_shape=(
            jax.ShapeDtypeStruct((own, length, channels), jnp.float32),
            jax.ShapeDtypeStruct((own, length, channels), jnp.bfloat16),
            jax.ShapeDtypeStruct((length, head_count, length), jnp.bfloat16),
        ),
        in_specs=[in_vmem] * 7,
        out_specs=(in_vmem,) * 3,
        scratch_shapes=[
            pltpu.VMEM((own, length, channels), jnp.bfloat16),
            pltpu.VMEM((own, length, channels), jnp.bfloat16),
            pltpu.VMEM((row_count, span, own, tile_cols, channels), jnp.bfloat16),
            dma((row_count, span)),
            dma((row_count, span)),
            dma((row_count, span)),
            dma((col_count,)),
            dma((row_count,)),
            dma((row_count,)),
            dma((device_total // 2,)),
            dma((device_total // 2,)),
            dma((device_total // 2,)),
            dma((device_total // 2,)),
        ],
        compiler_params=pltpu.CompilerParams(
            collective_id=0, has_side_effects=True, vmem_limit_bytes=VMEM_LIMIT
        ),
        name="transition",
    )(
        pair_state,
        jnp.transpose(pair_state, (1, 0, 2)),
        gain_transition[None, :],
        hidden_weight,
        out_weight,
        gain_attention[None, :],
        bias_weight.T,
    )
    penalty = mask_penalty * (1 - residue_mask).astype(jnp.float32)
    same_chain = (chain_ids[:, None] == chain_ids[None, :]).astype(jnp.float32)
    bias_full = (
        jnp.transpose(bias_rows, (1, 0, 2)).astype(jnp.float32)
        + chain_weight[:, None, None] * same_chain[None]
        - penalty[None, :, None]
    ) * LOG2_E
    pieces = pl.pallas_call(
        functools.partial(attention_kernel, row_count, col_count),
        out_shape=jax.ShapeDtypeStruct((row_count, col_count, own, own, channels), jnp.bfloat16),
        in_specs=[in_vmem] * 8,
        out_specs=in_vmem,
        scratch_shapes=[
            pltpu.VMEM((own, length, channels), jnp.float32),
            pltpu.VMEM((own, device_total, own, channels), jnp.bfloat16),
            pltpu.VMEM((device_total, own, own, channels), jnp.bfloat16),
            pltpu.VMEM((device_total, own, own, channels), jnp.float32),
            pltpu.VMEM((row_count, col_count, own, own, channels), jnp.bfloat16),
            dma((device_total,)),
            dma((own, device_total)),
            dma((row_count, own)),
            dma((row_count, own)),
        ],
        compiler_params=pltpu.CompilerParams(
            collective_id=1, has_side_effects=True, vmem_limit_bytes=VMEM_LIMIT
        ),
        name="attention",
    )(
        carried,
        normed,
        bias_full,
        query_weight.T,
        key_weight,
        value_weight.T,
        gate_weight.T,
        output_weight,
    )
    pieces = pieces.reshape(row_count, tile_rows, own, channels)
    return jnp.transpose(pieces, (1, 0, 2, 3)).reshape(tile_rows, tile_cols, channels)


def per_device(pair_state, *others):
    tile_cols = pair_state.shape[1]
    row_count, col_count = lax.axis_size("row"), lax.axis_size("col")
    own = tile_cols // row_count
    if own % 8 == 0 and col_count % 2 == 0 and col_count % row_count == 0:
        return owned_columns(pair_state, *others)
    return tile_layout(pair_state, *others)


def solution(mesh):
    placed = (
        P("row", "col", None),
        P(),
        P(),
        P(),
        P(),
        P(),
        P(),
        P(),
        P(),
        P(),
        P(),
        P(),
        P(),
        P(),
    )
    return jax.shard_map(
        per_device, mesh=mesh, in_specs=placed, out_specs=P("row", "col", None), check_vma=False
    )
```

```python
import functools
import math

import jax
import jax.numpy as jnp
from jax import lax
from jax.experimental import pallas as pl
from jax.experimental.pallas import tpu as pltpu
from jax.sharding import PartitionSpec as P

MESH = pl.DeviceIdType.MESH
VMEM_LIMIT = 60 * 1024 * 1024
LOG2_E = math.log2(math.e)

mask_penalty = 1000000000.0
norm_epsilon = 1e-05


def normalize(values, gain):
    center = values - jnp.mean(values, axis=-1, keepdims=True)
    variance = jnp.mean(center * center, axis=-1, keepdims=True)
    return center * lax.rsqrt(variance + norm_epsilon) * gain


def mirror(tile):
    tile_rows, tile_cols, channels = tile.shape
    col_count = lax.axis_size("col")
    row_count = lax.axis_size("row")
    col_ratio = col_count // row_count
    piece_len = tile_cols * tile_cols // col_count
    sectioned = tile.reshape(col_ratio, col_count, piece_len, channels)
    sectioned = lax.all_to_all(sectioned, "col", split_axis=1, concat_axis=1, tiled=True)
    sectioned = sectioned.reshape(col_ratio, row_count, col_ratio, piece_len, channels)
    sectioned = lax.all_to_all(sectioned, "row", split_axis=1, concat_axis=1, tiled=True)
    sectioned = jnp.transpose(sectioned, (1, 0, 2, 3, 4)).reshape(
        col_count, col_ratio, piece_len, channels
    )
    sectioned = lax.all_to_all(sectioned, "col", split_axis=0, concat_axis=0, tiled=True)
    sectioned = jnp.transpose(sectioned, (1, 0, 2, 3)).reshape(
        col_ratio, tile_cols, tile_cols, channels
    )
    return jnp.transpose(sectioned, (0, 2, 1, 3)).reshape(tile_rows, tile_cols, channels)


def attend(query_part, gate_part, key_part, value_part, bias_part, head_count, output_weight):
    query_total = query_part.shape[0]
    key_total = key_part.shape[0]
    head_dim = query_part.shape[1] // head_count
    score_scale = 1.0 / math.sqrt(head_dim)
    query_heads = query_part.reshape(query_total, head_count, head_dim)
    key_heads = key_part.reshape(key_total, head_count, head_dim)
    value_heads = value_part.reshape(key_total, head_count, head_dim)
    scores = (
        jnp.einsum("jhd,khd->hjk", query_heads, key_heads, preferred_element_type=jnp.float32)
        * score_scale
        + bias_part
    )
    row_max = jnp.max(scores, axis=-1, keepdims=True)
    exponent = jnp.exp(scores - row_max)
    attn_weights = (exponent / jnp.sum(exponent, axis=-1, keepdims=True)).astype(jnp.bfloat16)
    mixture = jnp.einsum(
        "hjk,khd->jhd", attn_weights, value_heads, preferred_element_type=jnp.float32
    )
    gated = (gate_part * mixture.reshape(query_total, head_count * head_dim)).astype(jnp.bfloat16)
    return jnp.dot(gated, output_weight, preferred_element_type=jnp.float32).astype(jnp.bfloat16)


def mirror_layout(
    normed_tile,
    bias_tile,
    chain_ids,
    penalty,
    chain_weight,
    query_weight,
    key_weight,
    value_weight,
    gate_weight,
    output_weight,
):
    tile_rows, tile_cols, channels = normed_tile.shape
    head_count = bias_tile.shape[0]
    row_start = lax.axis_index("row") * tile_rows
    flat_tile = normed_tile.reshape(tile_rows * tile_cols, channels)
    key_tile = (
        jnp.dot(flat_tile, key_weight, preferred_element_type=jnp.float32)
        .astype(jnp.bfloat16)
        .reshape(tile_rows, tile_cols, -1)
    )
    value_tile = (
        jnp.dot(flat_tile, value_weight, preferred_element_type=jnp.float32)
        .astype(jnp.bfloat16)
        .reshape(tile_rows, tile_cols, -1)
    )
    key_all, value_all = (
        lax.all_gather(key_tile, "row", axis=0, tiled=True),
        lax.all_gather(value_tile, "row", axis=0, tiled=True),
    )
    bias_rows = lax.all_gather(bias_tile, "col", axis=2, tiled=True)
    chain_rows = lax.dynamic_slice_in_dim(chain_ids, row_start, tile_rows, 0)
    same_chain = (chain_rows[:, None] == chain_ids[None, :]).astype(jnp.float32)
    bias_full = (
        bias_rows.astype(jnp.float32)
        + chain_weight[:, None, None] * same_chain[None]
        - penalty[None, None, :]
    )
    query_tile = (
        jnp.dot(flat_tile, query_weight, preferred_element_type=jnp.float32)
        .astype(jnp.bfloat16)
        .reshape(tile_rows, tile_cols, -1)
    )
    gate_tile = jax.nn.sigmoid(
        jnp.dot(flat_tile, gate_weight, preferred_element_type=jnp.float32)
    ).reshape(tile_rows, tile_cols, -1)

    def one_column(position):
        query_part = lax.dynamic_index_in_dim(query_tile, position, 1, keepdims=False)
        gate_part = lax.dynamic_index_in_dim(gate_tile, position, 1, keepdims=False)
        key_part = lax.dynamic_index_in_dim(key_all, position, 1, keepdims=False)
        value_part = lax.dynamic_index_in_dim(value_all, position, 1, keepdims=False)
        return attend(
            query_part, gate_part, key_part, value_part, bias_full, head_count, output_weight
        )

    results = lax.map(one_column, jnp.arange(tile_cols, dtype=jnp.int32))
    return jnp.transpose(results, (1, 0, 2))


def tile_layout(
    pair_state,
    residue_mask,
    chain_ids,
    gain_transition,
    hidden_weight,
    out_weight,
    gain_attention,
    query_weight,
    key_weight,
    value_weight,
    gate_weight,
    bias_weight,
    chain_weight,
    output_weight,
):
    tile_rows, tile_cols, channels = pair_state.shape
    head_count = chain_weight.shape[0]
    mirrored = mirror(pair_state)
    sym_tile = pair_state.astype(jnp.float32) + mirrored.astype(jnp.float32)
    flat_sym = sym_tile.reshape(tile_rows * tile_cols, channels)
    first_norm = normalize(flat_sym, gain_transition).astype(jnp.bfloat16)
    hidden_act = jax.nn.relu(
        jnp.dot(first_norm, hidden_weight, preferred_element_type=jnp.float32)
    ).astype(jnp.bfloat16)
    carried = flat_sym + jnp.dot(hidden_act, out_weight, preferred_element_type=jnp.float32)
    normed = normalize(carried, gain_attention).astype(jnp.bfloat16)
    bias_tile = (
        jnp.einsum("pd,dh->hp", normed, bias_weight, preferred_element_type=jnp.float32)
        .astype(jnp.bfloat16)
        .reshape(head_count, tile_rows, tile_cols)
    )
    penalty = mask_penalty * (1 - residue_mask).astype(jnp.float32)
    normed_tile = normed.reshape(tile_rows, tile_cols, channels)
    arguments = (
        normed_tile,
        bias_tile,
        chain_ids,
        penalty,
        chain_weight,
        query_weight,
        key_weight,
        value_weight,
        gate_weight,
        output_weight,
    )
    own_update = mirror_layout(*arguments)
    other_update = mirror(own_update)
    total = (
        2.0 * carried.reshape(tile_rows, tile_cols, channels)
        + own_update.astype(jnp.float32)
        + other_update.astype(jnp.float32)
    )
    return total.astype(jnp.bfloat16)


def greet_all(row_count, col_count):
    device_total = row_count * col_count
    me = lax.axis_index("col") * row_count + lax.axis_index("row")
    barrier = pltpu.get_barrier_semaphore()

    def greet(step, carry):
        peer = lax.rem(me + step, device_total)
        pl.semaphore_signal(
            barrier,
            inc=1,
            device_id=(lax.rem(peer, row_count), peer // row_count),
            device_id_type=MESH,
        )
        return carry

    lax.fori_loop(1, device_total, greet, 0)
    pl.semaphore_wait(barrier, device_total - 1)


def transition_kernel(
    row_count,
    col_count,
    tile_ref,
    turned_ref,
    gain_transition_ref,
    hidden_weight_ref,
    out_weight_ref,
    gain_attention_ref,
    bias_weight_ref,
    carried_ref,
    normed_ref,
    bias_ref,
    row_buf,
    col_buf,
    relay_buf,
    relay_send,
    relay_recv,
    row_send,
    row_recv,
    col_send,
    col_recv,
    bias_send,
    bias_recv,
    pair_send,
    pair_recv,
):
    tile_rows, tile_cols, channels = tile_ref.shape
    own = tile_cols // row_count
    span = col_count // row_count
    chip_total = row_count * col_count // 2
    row_id, col_id = lax.axis_index("row"), lax.axis_index("col")
    me = col_id * row_count + row_id
    side = lax.rem(col_id, 2)
    chip = (col_id // 2) * row_count + row_id
    greet_all(row_count, col_count)

    def relay_copy(other, slot):
        return pltpu.make_async_remote_copy(
            src_ref=tile_ref.at[pl.ds((slot * row_count + other) * own, own)],
            dst_ref=relay_buf.at[row_id, slot],
            send_sem=relay_send.at[other, slot],
            recv_sem=relay_recv.at[row_id, slot],
            device_id=(other, col_id),
            device_id_type=MESH,
        )

    def start_rows(origin, slot, source):
        target = origin * span + slot
        landing = row_buf.at[:, pl.ds(pl.multiple_of(col_id * tile_cols, tile_cols), tile_cols), :]

        @pl.when(target != col_id)
        def _():
            pltpu.make_async_remote_copy(
                src_ref=source,
                dst_ref=landing,
                send_sem=row_send.at[origin, slot],
                recv_sem=row_recv.at[col_id],
                device_id=(row_id, target),
                device_id_type=MESH,
            ).start()

        @pl.when(target == col_id)
        def _():
            pltpu.make_async_copy(source, landing, row_recv.at[col_id]).start()

    def col_remote(other):
        return pltpu.make_async_remote_copy(
            src_ref=turned_ref.at[pl.ds(other * own, own)],
            dst_ref=col_buf.at[
                :, pl.ds(pl.multiple_of(row_id * tile_rows, tile_rows), tile_rows), :
            ],
            send_sem=col_send.at[other],
            recv_sem=col_recv.at[row_id],
            device_id=(other, col_id),
            device_id_type=MESH,
        )

    def over_rows(body):
        def one(step, carry):
            body(lax.rem(row_id + step, row_count))
            return carry

        lax.fori_loop(1, row_count, one, 0)

    def over_slots(body):
        def one(step, carry):
            body(lax.rem(col_id + step, span))
            return carry

        lax.fori_loop(0, span, one, 0)

    over_rows(lambda other: over_slots(lambda slot: relay_copy(other, slot).start()))
    over_slots(
        lambda slot: start_rows(
            row_id, slot, tile_ref.at[pl.ds((slot * row_count + row_id) * own, own)]
        )
    )
    over_rows(lambda other: col_remote(other).start())
    own_col = pltpu.make_async_copy(
        turned_ref.at[pl.ds(row_id * own, own)],
        col_buf.at[:, pl.ds(pl.multiple_of(row_id * tile_rows, tile_rows), tile_rows), :],
        col_recv.at[row_id],
    )
    own_col.start()

    def pass_on(origin, slot):
        arrived = relay_buf.at[origin, slot]
        pltpu.make_async_copy(arrived, arrived, relay_recv.at[origin, slot]).wait()
        start_rows(origin, slot, arrived)

    over_rows(lambda origin: over_slots(lambda slot: pass_on(origin, slot)))

    def wait_row(other, carry):
        landed = row_buf.at[:, pl.ds(pl.multiple_of(other * tile_cols, tile_cols), tile_cols), :]
        pltpu.make_async_copy(landed, landed, row_recv.at[other]).wait()
        return carry

    lax.fori_loop(0, col_count, wait_row, 0)

    def wait_col(other, carry):
        landed = col_buf.at[:, pl.ds(pl.multiple_of(other * tile_rows, tile_rows), tile_rows), :]
        pltpu.make_async_copy(landed, landed, col_recv.at[other]).wait()
        return carry

    lax.fori_loop(0, row_count, wait_col, 0)

    def over_chips(body):
        def one(step, carry):
            body(lax.rem(chip + step, chip_total))
            return carry

        lax.fori_loop(1, chip_total, one, 0)

    def chip_place(other, which):
        return lax.rem(other, row_count), (other // row_count) * 2 + which

    def slab(other, which):
        place = chip_place(other, which)
        return bias_ref.at[pl.ds((place[1] * row_count + place[0]) * own, own)]

    def one_row(position, carry):
        sym_row = row_buf[position].astype(jnp.float32) + col_buf[position].astype(jnp.float32)
        first_norm = normalize(sym_row, gain_transition_ref[...]).astype(jnp.bfloat16)
        hidden_act = jax.nn.relu(
            jnp.dot(first_norm, hidden_weight_ref[...], preferred_element_type=jnp.float32)
        ).astype(jnp.bfloat16)
        carried = sym_row + jnp.dot(
            hidden_act, out_weight_ref[...], preferred_element_type=jnp.float32
        )
        carried_ref[position] = carried
        normed = normalize(carried, gain_attention_ref[...]).astype(jnp.bfloat16)
        normed_ref[position] = normed
        bias_ref[me * own + position] = lax.dot_general(
            bias_weight_ref[...],
            normed,
            (((1,), (1,)), ((), ())),
            preferred_element_type=jnp.float32,
        ).astype(jnp.bfloat16)
        over_chips(
            lambda other: pltpu.make_async_remote_copy(
                src_ref=bias_ref.at[me * own + position],
                dst_ref=bias_ref.at[me * own + position],
                send_sem=bias_send.at[other],
                recv_sem=bias_recv.at[chip],
                device_id=chip_place(other, side),
                device_id_type=MESH,
            ).start()
        )
        return carry

    lax.fori_loop(0, own, one_row, 0)

    def to_pair(other):
        return pltpu.make_async_remote_copy(
            src_ref=slab(other, side),
            dst_ref=slab(other, side),
            send_sem=pair_send.at[other],
            recv_sem=pair_recv.at[other],
            device_id=(row_id, col_id + 1 - 2 * side),
            device_id_type=MESH,
        )

    to_pair(chip).start()

    def hand_over(other):
        landed = slab(other, side)
        pltpu.make_async_copy(landed, landed, bias_recv.at[other]).wait()
        to_pair(other).start()

    over_chips(hand_over)

    def close_pair(other, carry):
        landed = slab(other, 1 - side)
        pltpu.make_async_copy(landed, landed, pair_recv.at[other]).wait()
        to_pair(other).wait_send()
        return carry

    lax.fori_loop(0, chip_total, close_pair, 0)

    def close_chip(other):
        sent = slab(chip, side)
        pltpu.make_async_copy(sent, sent, bias_send.at[other]).wait()

    over_chips(close_chip)

    def close_rows(origin, slot):
        @pl.when(origin * span + slot != col_id)
        def _():
            sent = relay_buf.at[origin, slot]
            pltpu.make_async_copy(sent, sent, row_send.at[origin, slot]).wait()

    over_slots(lambda slot: close_rows(row_id, slot))
    over_rows(lambda origin: over_slots(lambda slot: close_rows(origin, slot)))
    over_rows(lambda other: over_slots(lambda slot: relay_copy(other, slot).wait_send()))
    over_rows(lambda other: col_remote(other).wait_send())


def attention_kernel(
    row_count,
    col_count,
    carried_ref,
    normed_ref,
    bias_ref,
    query_turned_ref,
    key_weight_ref,
    value_turned_ref,
    gate_turned_ref,
    output_weight_ref,
    out_ref,
    total,
    update_buf,
    recv_buf,
    turned,
    sum_buf,
    score_buf,
    weight_buf,
    update_send,
    update_recv,
    sum_send,
    sum_recv,
):
    own, length, channels = normed_ref.shape
    head_count = bias_ref.shape[0]
    inner_total = key_weight_ref.shape[1]
    head_dim = inner_total // head_count
    score_scale = LOG2_E / math.sqrt(head_dim)
    device_total = row_count * col_count
    row_id, col_id = lax.axis_index("row"), lax.axis_index("col")
    me = col_id * row_count + row_id
    greet_all(row_count, col_count)

    def over_peers(body):
        def one(step, carry):
            body(lax.rem(me + step, device_total))
            return carry

        lax.fori_loop(1, device_total, one, 0)

    def over_rows(body):
        def one(step, carry):
            body(lax.rem(row_id + step, row_count))
            return carry

        lax.fori_loop(1, row_count, one, 0)

    strip = min(128, length)
    band = min(inner_total, max(128, head_dim))
    heads_in_band = band // head_dim
    head_of_lane = lax.broadcasted_iota(jnp.int32, (1, band), 1) // head_dim

    def one_row(position, carry):
        normed = normed_ref[position]
        normed_turned = normed.T

        def project(weight_ref):
            return jnp.dot(weight_ref[...], normed_turned, preferred_element_type=jnp.float32)

        keys = jnp.dot(
            normed, key_weight_ref[...], preferred_element_type=jnp.float32
        ).astype(jnp.bfloat16)
        queries = project(query_turned_ref).astype(jnp.bfloat16)
        values = project(value_turned_ref).astype(jnp.bfloat16)
        gates = jax.nn.sigmoid(project(gate_turned_ref))
        for head in range(head_count):
            first = head // heads_in_band * band
            chosen = (head_of_lane == head % heads_in_band).astype(jnp.bfloat16)
            score_buf[head] = (
                jnp.dot(
                    keys[:, first : first + band] * chosen,
                    queries[first : first + band],
                    preferred_element_type=jnp.float32,
                )
                * score_scale
                + bias_ref[head]
            )
        mixed = []
        for head in range(head_count):
            rows = slice(head * head_dim, (head + 1) * head_dim)
            for start in range(0, length, strip):
                places = slice(start, start + strip)
                scores = score_buf[head, :, places]
                exponent = jnp.exp2(scores - jnp.max(scores, axis=0, keepdims=True))
                weight_buf[head, :, places] = (
                    exponent * (1.0 / jnp.sum(exponent, axis=0, keepdims=True))
                ).astype(jnp.bfloat16)
            mixture = jnp.dot(values[rows], weight_buf[head], preferred_element_type=jnp.float32)
            mixed.append((gates[rows] * mixture).astype(jnp.bfloat16))
        gated = jnp.concatenate(mixed, axis=0).T
        update = jnp.dot(gated, output_weight_ref[...], preferred_element_type=jnp.float32)
        update = update.reshape(device_total, own, channels).astype(jnp.bfloat16)
        update_buf[position] = update
        recv_buf[me, position] = update_buf[position, me]
        total[position] = 2.0 * carried_ref[position] + update.astype(jnp.float32).reshape(
            length, channels
        )
        over_peers(
            lambda peer: pltpu.make_async_remote_copy(
                src_ref=update_buf.at[position, peer],
                dst_ref=recv_buf.at[me, position],
                send_sem=update_send.at[peer],
                recv_sem=update_recv.at[position, me],
                device_id=(lax.rem(peer, row_count), peer // row_count),
                device_id_type=MESH,
            ).start()
        )
        return carry

    lax.fori_loop(0, own, one_row, 0)
    for position in range(own):
        turned[:, :, position, :] = total[position].reshape(device_total, own, channels)

    def summed(other, position):
        devices = pl.ds(other * col_count, col_count)
        return (
            turned[devices, position] + recv_buf[devices, position].astype(jnp.float32)
        ).astype(jnp.bfloat16)

    def sum_remote(other, position):
        return pltpu.make_async_remote_copy(
            src_ref=sum_buf.at[other, :, position],
            dst_ref=out_ref.at[row_id, :, position],
            send_sem=sum_send.at[other, position],
            recv_sem=sum_recv.at[row_id, position],
            device_id=(other, col_id),
            device_id_type=MESH,
        )

    def finish_position(position, carry):
        def arrived(peer):
            landed = recv_buf.at[peer, position]
            pltpu.make_async_copy(landed, landed, update_recv.at[position, peer]).wait()

        over_peers(arrived)

        def pass_sum(other):
            sum_buf[other, :, position] = summed(other, position)
            sum_remote(other, position).start()

        over_rows(pass_sum)
        out_ref[row_id, :, position] = summed(row_id, position)
        return carry

    lax.fori_loop(0, own, finish_position, 0)

    def close_peer(peer):
        sent = recv_buf.at[peer]
        pltpu.make_async_copy(sent, sent, update_send.at[peer]).wait()

    over_peers(close_peer)

    def close_position(position, carry):
        def close_row(other):
            landed = out_ref.at[other, :, position]
            pltpu.make_async_copy(landed, landed, sum_recv.at[other, position]).wait()
            sum_remote(other, position).wait_send()

        over_rows(close_row)
        return carry

    lax.fori_loop(0, own, close_position, 0)


def owned_columns(
    pair_state,
    residue_mask,
    chain_ids,
    gain_transition,
    hidden_weight,
    out_weight,
    gain_attention,
    query_weight,
    key_weight,
    value_weight,
    gate_weight,
    bias_weight,
    chain_weight,
    output_weight,
):
    tile_rows, tile_cols, channels = pair_state.shape
    row_count, col_count = lax.axis_size("row"), lax.axis_size("col")
    device_total = row_count * col_count
    head_count = chain_weight.shape[0]
    length = tile_rows * row_count
    own = tile_cols // row_count
    span = col_count // row_count
    in_vmem = pl.BlockSpec(memory_space=pltpu.VMEM)
    dma = pltpu.SemaphoreType.DMA
    carried, normed, bias_rows = pl.pallas_call(
        functools.partial(transition_kernel, row_count, col_count),
        out_shape=(
            jax.ShapeDtypeStruct((own, length, channels), jnp.float32),
            jax.ShapeDtypeStruct((own, length, channels), jnp.bfloat16),
            jax.ShapeDtypeStruct((length, head_count, length), jnp.bfloat16),
        ),
        in_specs=[in_vmem] * 7,
        out_specs=(in_vmem,) * 3,
        scratch_shapes=[
            pltpu.VMEM((own, length, channels), jnp.bfloat16),
            pltpu.VMEM((own, length, channels), jnp.bfloat16),
            pltpu.VMEM((row_count, span, own, tile_cols, channels), jnp.bfloat16),
            dma((row_count, span)),
            dma((row_count, span)),
            dma((row_count, span)),
            dma((col_count,)),
            dma((row_count,)),
            dma((row_count,)),
            dma((device_total // 2,)),
            dma((device_total // 2,)),
            dma((device_total // 2,)),
            dma((device_total // 2,)),
        ],
        compiler_params=pltpu.CompilerParams(
            collective_id=0, has_side_effects=True, vmem_limit_bytes=VMEM_LIMIT
        ),
        name="transition",
    )(
        pair_state,
        jnp.transpose(pair_state, (1, 0, 2)),
        gain_transition[None, :],
        hidden_weight,
        out_weight,
        gain_attention[None, :],
        bias_weight.T,
    )
    penalty = mask_penalty * (1 - residue_mask).astype(jnp.float32)
    same_chain = (chain_ids[:, None] == chain_ids[None, :]).astype(jnp.float32)
    bias_full = (
        jnp.transpose(bias_rows, (1, 0, 2)).astype(jnp.float32)
        + chain_weight[:, None, None] * same_chain[None]
        - penalty[None, :, None]
    ) * LOG2_E
    pieces = pl.pallas_call(
        functools.partial(attention_kernel, row_count, col_count),
        out_shape=jax.ShapeDtypeStruct((row_count, col_count, own, own, channels), jnp.bfloat16),
        in_specs=[in_vmem] * 8,
        out_specs=in_vmem,
        scratch_shapes=[
            pltpu.VMEM((own, length, channels), jnp.float32),
            pltpu.VMEM((own, device_total, own, channels), jnp.bfloat16),
            pltpu.VMEM((device_total, own, own, channels), jnp.bfloat16),
            pltpu.VMEM((device_total, own, own, channels), jnp.float32),
            pltpu.VMEM((row_count, col_count, own, own, channels), jnp.bfloat16),
            pltpu.VMEM((head_count, length, length), jnp.float32),
            pltpu.VMEM((head_count, length, length), jnp.bfloat16),
            dma((device_total,)),
            dma((own, device_total)),
            dma((row_count, own)),
            dma((row_count, own)),
        ],
        compiler_params=pltpu.CompilerParams(
            collective_id=1, has_side_effects=True, vmem_limit_bytes=VMEM_LIMIT
        ),
        name="attention",
    )(
        carried,
        normed,
        bias_full,
        query_weight.T,
        key_weight,
        value_weight.T,
        gate_weight.T,
        output_weight,
    )
    pieces = pieces.reshape(row_count, tile_rows, own, channels)
    return jnp.transpose(pieces, (1, 0, 2, 3)).reshape(tile_rows, tile_cols, channels)


def per_device(pair_state, *others):
    tile_cols = pair_state.shape[1]
    row_count, col_count = lax.axis_size("row"), lax.axis_size("col")
    own = tile_cols // row_count
    if own % 8 == 0 and col_count % 2 == 0 and col_count % row_count == 0:
        return owned_columns(pair_state, *others)
    return tile_layout(pair_state, *others)


def solution(mesh):
    placed = (
        P("row", "col", None),
        P(),
        P(),
        P(),
        P(),
        P(),
        P(),
        P(),
        P(),
        P(),
        P(),
        P(),
        P(),
        P(),
    )
    return jax.shard_map(
        per_device, mesh=mesh, in_specs=placed, out_specs=P("row", "col", None), check_vma=False
    )
```

```python
import functools
import math

import jax
import jax.numpy as jnp
from jax import lax
from jax.experimental import pallas as pl
from jax.experimental.pallas import tpu as pltpu
from jax.sharding import PartitionSpec as P

MESH = pl.DeviceIdType.MESH
VMEM_LIMIT = 60 * 1024 * 1024
LOG2_E = math.log2(math.e)

mask_penalty = 1000000000.0
norm_epsilon = 1e-05


def normalize(values, gain):
    center = values - jnp.mean(values, axis=-1, keepdims=True)
    variance = jnp.mean(center * center, axis=-1, keepdims=True)
    return center * lax.rsqrt(variance + norm_epsilon) * gain


def mirror(tile):
    tile_rows, tile_cols, channels = tile.shape
    col_count = lax.axis_size("col")
    row_count = lax.axis_size("row")
    col_ratio = col_count // row_count
    piece_len = tile_cols * tile_cols // col_count
    sectioned = tile.reshape(col_ratio, col_count, piece_len, channels)
    sectioned = lax.all_to_all(sectioned, "col", split_axis=1, concat_axis=1, tiled=True)
    sectioned = sectioned.reshape(col_ratio, row_count, col_ratio, piece_len, channels)
    sectioned = lax.all_to_all(sectioned, "row", split_axis=1, concat_axis=1, tiled=True)
    sectioned = jnp.transpose(sectioned, (1, 0, 2, 3, 4)).reshape(
        col_count, col_ratio, piece_len, channels
    )
    sectioned = lax.all_to_all(sectioned, "col", split_axis=0, concat_axis=0, tiled=True)
    sectioned = jnp.transpose(sectioned, (1, 0, 2, 3)).reshape(
        col_ratio, tile_cols, tile_cols, channels
    )
    return jnp.transpose(sectioned, (0, 2, 1, 3)).reshape(tile_rows, tile_cols, channels)


def attend(query_part, gate_part, key_part, value_part, bias_part, head_count, output_weight):
    query_total = query_part.shape[0]
    key_total = key_part.shape[0]
    head_dim = query_part.shape[1] // head_count
    score_scale = 1.0 / math.sqrt(head_dim)
    query_heads = query_part.reshape(query_total, head_count, head_dim)
    key_heads = key_part.reshape(key_total, head_count, head_dim)
    value_heads = value_part.reshape(key_total, head_count, head_dim)
    scores = (
        jnp.einsum("jhd,khd->hjk", query_heads, key_heads, preferred_element_type=jnp.float32)
        * score_scale
        + bias_part
    )
    row_max = jnp.max(scores, axis=-1, keepdims=True)
    exponent = jnp.exp(scores - row_max)
    attn_weights = (exponent / jnp.sum(exponent, axis=-1, keepdims=True)).astype(jnp.bfloat16)
    mixture = jnp.einsum(
        "hjk,khd->jhd", attn_weights, value_heads, preferred_element_type=jnp.float32
    )
    gated = (gate_part * mixture.reshape(query_total, head_count * head_dim)).astype(jnp.bfloat16)
    return jnp.dot(gated, output_weight, preferred_element_type=jnp.float32).astype(jnp.bfloat16)


def mirror_layout(
    normed_tile,
    bias_tile,
    chain_ids,
    penalty,
    chain_weight,
    query_weight,
    key_weight,
    value_weight,
    gate_weight,
    output_weight,
):
    tile_rows, tile_cols, channels = normed_tile.shape
    head_count = bias_tile.shape[0]
    row_start = lax.axis_index("row") * tile_rows
    flat_tile = normed_tile.reshape(tile_rows * tile_cols, channels)
    key_tile = (
        jnp.dot(flat_tile, key_weight, preferred_element_type=jnp.float32)
        .astype(jnp.bfloat16)
        .reshape(tile_rows, tile_cols, -1)
    )
    value_tile = (
        jnp.dot(flat_tile, value_weight, preferred_element_type=jnp.float32)
        .astype(jnp.bfloat16)
        .reshape(tile_rows, tile_cols, -1)
    )
    key_all, value_all = (
        lax.all_gather(key_tile, "row", axis=0, tiled=True),
        lax.all_gather(value_tile, "row", axis=0, tiled=True),
    )
    bias_rows = lax.all_gather(bias_tile, "col", axis=2, tiled=True)
    chain_rows = lax.dynamic_slice_in_dim(chain_ids, row_start, tile_rows, 0)
    same_chain = (chain_rows[:, None] == chain_ids[None, :]).astype(jnp.float32)
    bias_full = (
        bias_rows.astype(jnp.float32)
        + chain_weight[:, None, None] * same_chain[None]
        - penalty[None, None, :]
    )
    query_tile = (
        jnp.dot(flat_tile, query_weight, preferred_element_type=jnp.float32)
        .astype(jnp.bfloat16)
        .reshape(tile_rows, tile_cols, -1)
    )
    gate_tile = jax.nn.sigmoid(
        jnp.dot(flat_tile, gate_weight, preferred_element_type=jnp.float32)
    ).reshape(tile_rows, tile_cols, -1)

    def one_column(position):
        query_part = lax.dynamic_index_in_dim(query_tile, position, 1, keepdims=False)
        gate_part = lax.dynamic_index_in_dim(gate_tile, position, 1, keepdims=False)
        key_part = lax.dynamic_index_in_dim(key_all, position, 1, keepdims=False)
        value_part = lax.dynamic_index_in_dim(value_all, position, 1, keepdims=False)
        return attend(
            query_part, gate_part, key_part, value_part, bias_full, head_count, output_weight
        )

    results = lax.map(one_column, jnp.arange(tile_cols, dtype=jnp.int32))
    return jnp.transpose(results, (1, 0, 2))


def tile_layout(
    pair_state,
    residue_mask,
    chain_ids,
    gain_transition,
    hidden_weight,
    out_weight,
    gain_attention,
    query_weight,
    key_weight,
    value_weight,
    gate_weight,
    bias_weight,
    chain_weight,
    output_weight,
):
    tile_rows, tile_cols, channels = pair_state.shape
    head_count = chain_weight.shape[0]
    mirrored = mirror(pair_state)
    sym_tile = pair_state.astype(jnp.float32) + mirrored.astype(jnp.float32)
    flat_sym = sym_tile.reshape(tile_rows * tile_cols, channels)
    first_norm = normalize(flat_sym, gain_transition).astype(jnp.bfloat16)
    hidden_act = jax.nn.relu(
        jnp.dot(first_norm, hidden_weight, preferred_element_type=jnp.float32)
    ).astype(jnp.bfloat16)
    carried = flat_sym + jnp.dot(hidden_act, out_weight, preferred_element_type=jnp.float32)
    normed = normalize(carried, gain_attention).astype(jnp.bfloat16)
    bias_tile = (
        jnp.einsum("pd,dh->hp", normed, bias_weight, preferred_element_type=jnp.float32)
        .astype(jnp.bfloat16)
        .reshape(head_count, tile_rows, tile_cols)
    )
    penalty = mask_penalty * (1 - residue_mask).astype(jnp.float32)
    normed_tile = normed.reshape(tile_rows, tile_cols, channels)
    arguments = (
        normed_tile,
        bias_tile,
        chain_ids,
        penalty,
        chain_weight,
        query_weight,
        key_weight,
        value_weight,
        gate_weight,
        output_weight,
    )
    own_update = mirror_layout(*arguments)
    other_update = mirror(own_update)
    total = (
        2.0 * carried.reshape(tile_rows, tile_cols, channels)
        + own_update.astype(jnp.float32)
        + other_update.astype(jnp.float32)
    )
    return total.astype(jnp.bfloat16)


def greet_all(row_count, col_count):
    device_total = row_count * col_count
    me = lax.axis_index("col") * row_count + lax.axis_index("row")
    barrier = pltpu.get_barrier_semaphore()

    def greet(step, carry):
        peer = lax.rem(me + step, device_total)
        pl.semaphore_signal(
            barrier,
            inc=1,
            device_id=(lax.rem(peer, row_count), peer // row_count),
            device_id_type=MESH,
        )
        return carry

    lax.fori_loop(1, device_total, greet, 0)
    pl.semaphore_wait(barrier, device_total - 1)


def transition_kernel(
    row_count,
    col_count,
    tile_ref,
    turned_ref,
    gain_transition_ref,
    hidden_weight_ref,
    out_weight_ref,
    gain_attention_ref,
    bias_weight_ref,
    carried_ref,
    normed_ref,
    bias_ref,
    row_buf,
    col_buf,
    relay_buf,
    relay_send,
    relay_recv,
    row_send,
    row_recv,
    col_send,
    col_recv,
    bias_send,
    bias_recv,
    pair_send,
    pair_recv,
):
    tile_rows, tile_cols, channels = tile_ref.shape
    own = tile_cols // row_count
    span = col_count // row_count
    chip_total = row_count * col_count // 2
    row_id, col_id = lax.axis_index("row"), lax.axis_index("col")
    me = col_id * row_count + row_id
    side = lax.rem(col_id, 2)
    chip = (col_id // 2) * row_count + row_id
    greet_all(row_count, col_count)

    def relay_copy(other, slot):
        return pltpu.make_async_remote_copy(
            src_ref=tile_ref.at[pl.ds((slot * row_count + other) * own, own)],
            dst_ref=relay_buf.at[row_id, slot],
            send_sem=relay_send.at[other, slot],
            recv_sem=relay_recv.at[row_id, slot],
            device_id=(other, col_id),
            device_id_type=MESH,
        )

    def start_rows(origin, slot, source):
        target = origin * span + slot
        landing = row_buf.at[:, pl.ds(pl.multiple_of(col_id * tile_cols, tile_cols), tile_cols), :]

        @pl.when(target != col_id)
        def _():
            pltpu.make_async_remote_copy(
                src_ref=source,
                dst_ref=landing,
                send_sem=row_send.at[origin, slot],
                recv_sem=row_recv.at[col_id],
                device_id=(row_id, target),
                device_id_type=MESH,
            ).start()

        @pl.when(target == col_id)
        def _():
            pltpu.make_async_copy(source, landing, row_recv.at[col_id]).start()

    def col_remote(other):
        return pltpu.make_async_remote_copy(
            src_ref=turned_ref.at[pl.ds(other * own, own)],
            dst_ref=col_buf.at[
                :, pl.ds(pl.multiple_of(row_id * tile_rows, tile_rows), tile_rows), :
            ],
            send_sem=col_send.at[other],
            recv_sem=col_recv.at[row_id],
            device_id=(other, col_id),
            device_id_type=MESH,
        )

    def over_rows(body):
        def one(step, carry):
            body(lax.rem(row_id + step, row_count))
            return carry

        lax.fori_loop(1, row_count, one, 0)

    def over_slots(body):
        def one(step, carry):
            body(lax.rem(col_id + step, span))
            return carry

        lax.fori_loop(0, span, one, 0)

    over_rows(lambda other: over_slots(lambda slot: relay_copy(other, slot).start()))
    over_slots(
        lambda slot: start_rows(
            row_id, slot, tile_ref.at[pl.ds((slot * row_count + row_id) * own, own)]
        )
    )
    over_rows(lambda other: col_remote(other).start())
    own_col = pltpu.make_async_copy(
        turned_ref.at[pl.ds(row_id * own, own)],
        col_buf.at[:, pl.ds(pl.multiple_of(row_id * tile_rows, tile_rows), tile_rows), :],
        col_recv.at[row_id],
    )
    own_col.start()

    def pass_on(origin, slot):
        arrived = relay_buf.at[origin, slot]
        pltpu.make_async_copy(arrived, arrived, relay_recv.at[origin, slot]).wait()
        start_rows(origin, slot, arrived)

    over_rows(lambda origin: over_slots(lambda slot: pass_on(origin, slot)))

    def wait_row(other, carry):
        landed = row_buf.at[:, pl.ds(pl.multiple_of(other * tile_cols, tile_cols), tile_cols), :]
        pltpu.make_async_copy(landed, landed, row_recv.at[other]).wait()
        return carry

    lax.fori_loop(0, col_count, wait_row, 0)

    def wait_col(other, carry):
        landed = col_buf.at[:, pl.ds(pl.multiple_of(other * tile_rows, tile_rows), tile_rows), :]
        pltpu.make_async_copy(landed, landed, col_recv.at[other]).wait()
        return carry

    lax.fori_loop(0, row_count, wait_col, 0)

    def over_chips(body):
        def one(step, carry):
            body(lax.rem(chip + step, chip_total))
            return carry

        lax.fori_loop(1, chip_total, one, 0)

    def chip_place(other, which):
        return lax.rem(other, row_count), (other // row_count) * 2 + which

    def slab(other, which):
        place = chip_place(other, which)
        return bias_ref.at[pl.ds((place[1] * row_count + place[0]) * own, own)]

    def one_row(position, carry):
        sym_row = row_buf[position].astype(jnp.float32) + col_buf[position].astype(jnp.float32)
        first_norm = normalize(sym_row, gain_transition_ref[...]).astype(jnp.bfloat16)
        hidden_act = jax.nn.relu(
            jnp.dot(first_norm, hidden_weight_ref[...], preferred_element_type=jnp.float32)
        ).astype(jnp.bfloat16)
        carried = sym_row + jnp.dot(
            hidden_act, out_weight_ref[...], preferred_element_type=jnp.float32
        )
        carried_ref[position] = carried
        normed = normalize(carried, gain_attention_ref[...]).astype(jnp.bfloat16)
        normed_ref[position] = normed
        bias_ref[me * own + position] = lax.dot_general(
            bias_weight_ref[...],
            normed,
            (((1,), (1,)), ((), ())),
            preferred_element_type=jnp.float32,
        ).astype(jnp.bfloat16)
        over_chips(
            lambda other: pltpu.make_async_remote_copy(
                src_ref=bias_ref.at[me * own + position],
                dst_ref=bias_ref.at[me * own + position],
                send_sem=bias_send.at[other],
                recv_sem=bias_recv.at[chip],
                device_id=chip_place(other, side),
                device_id_type=MESH,
            ).start()
        )
        return carry

    lax.fori_loop(0, own, one_row, 0)

    def to_pair(other):
        return pltpu.make_async_remote_copy(
            src_ref=slab(other, side),
            dst_ref=slab(other, side),
            send_sem=pair_send.at[other],
            recv_sem=pair_recv.at[other],
            device_id=(row_id, col_id + 1 - 2 * side),
            device_id_type=MESH,
        )

    to_pair(chip).start()

    def hand_over(other):
        landed = slab(other, side)
        pltpu.make_async_copy(landed, landed, bias_recv.at[other]).wait()
        to_pair(other).start()

    over_chips(hand_over)

    def close_pair(other, carry):
        landed = slab(other, 1 - side)
        pltpu.make_async_copy(landed, landed, pair_recv.at[other]).wait()
        to_pair(other).wait_send()
        return carry

    lax.fori_loop(0, chip_total, close_pair, 0)

    def close_chip(other):
        sent = slab(chip, side)
        pltpu.make_async_copy(sent, sent, bias_send.at[other]).wait()

    over_chips(close_chip)

    def close_rows(origin, slot):
        @pl.when(origin * span + slot != col_id)
        def _():
            sent = relay_buf.at[origin, slot]
            pltpu.make_async_copy(sent, sent, row_send.at[origin, slot]).wait()

    over_slots(lambda slot: close_rows(row_id, slot))
    over_rows(lambda origin: over_slots(lambda slot: close_rows(origin, slot)))
    over_rows(lambda other: over_slots(lambda slot: relay_copy(other, slot).wait_send()))
    over_rows(lambda other: col_remote(other).wait_send())


def attention_kernel(
    row_count,
    col_count,
    carried_ref,
    normed_ref,
    bias_ref,
    query_weight_ref,
    key_weight_ref,
    value_weight_ref,
    gate_weight_ref,
    output_weight_ref,
    out_ref,
    total,
    update_buf,
    recv_buf,
    turned,
    sum_buf,
    score_buf,
    weight_buf,
    query_turned,
    value_turned,
    gate_turned,
    update_send,
    update_recv,
    sum_send,
    sum_recv,
):
    own, length, channels = normed_ref.shape
    head_count = bias_ref.shape[0]
    inner_total = key_weight_ref.shape[1]
    head_dim = inner_total // head_count
    score_scale = LOG2_E / math.sqrt(head_dim)
    device_total = row_count * col_count
    row_id, col_id = lax.axis_index("row"), lax.axis_index("col")
    me = col_id * row_count + row_id
    query_turned[...] = query_weight_ref[...].T
    value_turned[...] = value_weight_ref[...].T
    gate_turned[...] = gate_weight_ref[...].T
    greet_all(row_count, col_count)

    def over_peers(body):
        def one(step, carry):
            body(lax.rem(me + step, device_total))
            return carry

        lax.fori_loop(1, device_total, one, 0)

    def over_rows(body):
        def one(step, carry):
            body(lax.rem(row_id + step, row_count))
            return carry

        lax.fori_loop(1, row_count, one, 0)

    strip = min(128, length)
    band = min(inner_total, max(128, head_dim))
    heads_in_band = band // head_dim
    head_of_lane = lax.broadcasted_iota(jnp.int32, (1, band), 1) // head_dim

    def one_row(position, carry):
        normed = normed_ref[position]
        normed_turned = normed.T

        def project(weight_ref):
            return jnp.dot(weight_ref[...], normed_turned, preferred_element_type=jnp.float32)

        keys = jnp.dot(
            normed, key_weight_ref[...], preferred_element_type=jnp.float32
        ).astype(jnp.bfloat16)
        queries = project(query_turned).astype(jnp.bfloat16)
        values = project(value_turned).astype(jnp.bfloat16)
        gates = jax.nn.sigmoid(project(gate_turned))
        def score(head):
            first = head // heads_in_band * band
            chosen = (head_of_lane == head % heads_in_band).astype(jnp.bfloat16)
            score_buf[head] = (
                jnp.dot(
                    keys[:, first : first + band] * chosen,
                    queries[first : first + band],
                    preferred_element_type=jnp.float32,
                )
                * score_scale
                + bias_ref[head]
            )

        mixed = []
        for head in range(4):
            score(head)
        for head in range(head_count):
            if head + 4 < head_count:
                score(head + 4)
            rows = slice(head * head_dim, (head + 1) * head_dim)
            for start in range(0, length, strip):
                places = slice(start, start + strip)
                scores = score_buf[head, :, places]
                exponent = jnp.exp2(scores - jnp.max(scores, axis=0, keepdims=True))
                weight_buf[head, :, places] = (
                    exponent * (1.0 / jnp.sum(exponent, axis=0, keepdims=True))
                ).astype(jnp.bfloat16)
            mixture = jnp.dot(values[rows], weight_buf[head], preferred_element_type=jnp.float32)
            mixed.append((gates[rows] * mixture).astype(jnp.bfloat16))
        gated = jnp.concatenate(mixed, axis=0).T
        update = jnp.dot(gated, output_weight_ref[...], preferred_element_type=jnp.float32)
        update = update.reshape(device_total, own, channels).astype(jnp.bfloat16)
        update_buf[position] = update
        recv_buf[me, position] = update_buf[position, me]
        total[position] = 2.0 * carried_ref[position] + update.astype(jnp.float32).reshape(
            length, channels
        )
        over_peers(
            lambda peer: pltpu.make_async_remote_copy(
                src_ref=update_buf.at[position, peer],
                dst_ref=recv_buf.at[me, position],
                send_sem=update_send.at[peer],
                recv_sem=update_recv.at[position, me],
                device_id=(lax.rem(peer, row_count), peer // row_count),
                device_id_type=MESH,
            ).start()
        )
        return carry

    lax.fori_loop(0, own, one_row, 0)
    for position in range(own):
        turned[:, :, position, :] = total[position].reshape(device_total, own, channels)

    def summed(other, position):
        devices = pl.ds(other * col_count, col_count)
        return (
            turned[devices, position] + recv_buf[devices, position].astype(jnp.float32)
        ).astype(jnp.bfloat16)

    def sum_remote(other, position):
        return pltpu.make_async_remote_copy(
            src_ref=sum_buf.at[other, :, position],
            dst_ref=out_ref.at[row_id, :, position],
            send_sem=sum_send.at[other, position],
            recv_sem=sum_recv.at[row_id, position],
            device_id=(other, col_id),
            device_id_type=MESH,
        )

    def finish_position(position, carry):
        def arrived(peer):
            landed = recv_buf.at[peer, position]
            pltpu.make_async_copy(landed, landed, update_recv.at[position, peer]).wait()

        over_peers(arrived)

        def pass_sum(other):
            sum_buf[other, :, position] = summed(other, position)
            sum_remote(other, position).start()

        over_rows(pass_sum)
        out_ref[row_id, :, position] = summed(row_id, position)
        return carry

    lax.fori_loop(0, own, finish_position, 0)

    def close_peer(peer):
        sent = recv_buf.at[peer]
        pltpu.make_async_copy(sent, sent, update_send.at[peer]).wait()

    over_peers(close_peer)

    def close_position(position, carry):
        def close_row(other):
            landed = out_ref.at[other, :, position]
            pltpu.make_async_copy(landed, landed, sum_recv.at[other, position]).wait()
            sum_remote(other, position).wait_send()

        over_rows(close_row)
        return carry

    lax.fori_loop(0, own, close_position, 0)


def owned_columns(
    pair_state,
    residue_mask,
    chain_ids,
    gain_transition,
    hidden_weight,
    out_weight,
    gain_attention,
    query_weight,
    key_weight,
    value_weight,
    gate_weight,
    bias_weight,
    chain_weight,
    output_weight,
):
    tile_rows, tile_cols, channels = pair_state.shape
    row_count, col_count = lax.axis_size("row"), lax.axis_size("col")
    device_total = row_count * col_count
    head_count = chain_weight.shape[0]
    length = tile_rows * row_count
    own = tile_cols // row_count
    span = col_count // row_count
    in_vmem = pl.BlockSpec(memory_space=pltpu.VMEM)
    dma = pltpu.SemaphoreType.DMA
    carried, normed, bias_rows = pl.pallas_call(
        functools.partial(transition_kernel, row_count, col_count),
        out_shape=(
            jax.ShapeDtypeStruct((own, length, channels), jnp.float32),
            jax.ShapeDtypeStruct((own, length, channels), jnp.bfloat16),
            jax.ShapeDtypeStruct((length, head_count, length), jnp.bfloat16),
        ),
        in_specs=[in_vmem] * 7,
        out_specs=(in_vmem,) * 3,
        scratch_shapes=[
            pltpu.VMEM((own, length, channels), jnp.bfloat16),
            pltpu.VMEM((own, length, channels), jnp.bfloat16),
            pltpu.VMEM((row_count, span, own, tile_cols, channels), jnp.bfloat16),
            dma((row_count, span)),
            dma((row_count, span)),
            dma((row_count, span)),
            dma((col_count,)),
            dma((row_count,)),
            dma((row_count,)),
            dma((device_total // 2,)),
            dma((device_total // 2,)),
            dma((device_total // 2,)),
            dma((device_total // 2,)),
        ],
        compiler_params=pltpu.CompilerParams(
            collective_id=0, has_side_effects=True, vmem_limit_bytes=VMEM_LIMIT
        ),
        name="transition",
    )(
        pair_state,
        jnp.transpose(pair_state, (1, 0, 2)),
        gain_transition[None, :],
        hidden_weight,
        out_weight,
        gain_attention[None, :],
        bias_weight.T,
    )
    penalty = mask_penalty * (1 - residue_mask).astype(jnp.float32)
    same_chain = (chain_ids[:, None] == chain_ids[None, :]).astype(jnp.float32)
    bias_full = (
        jnp.transpose(bias_rows, (1, 0, 2)).astype(jnp.float32)
        + chain_weight[:, None, None] * same_chain[None]
        - penalty[None, :, None]
    ) * LOG2_E
    pieces = pl.pallas_call(
        functools.partial(attention_kernel, row_count, col_count),
        out_shape=jax.ShapeDtypeStruct((row_count, col_count, own, own, channels), jnp.bfloat16),
        in_specs=[in_vmem] * 8,
        out_specs=in_vmem,
        scratch_shapes=[
            pltpu.VMEM((own, length, channels), jnp.float32),
            pltpu.VMEM((own, device_total, own, channels), jnp.bfloat16),
            pltpu.VMEM((device_total, own, own, channels), jnp.bfloat16),
            pltpu.VMEM((device_total, own, own, channels), jnp.float32),
            pltpu.VMEM((row_count, col_count, own, own, channels), jnp.bfloat16),
            pltpu.VMEM((head_count, length, length), jnp.float32),
            pltpu.VMEM((head_count, length, length), jnp.bfloat16),
            pltpu.VMEM(query_weight.shape[::-1], jnp.bfloat16),
            pltpu.VMEM(value_weight.shape[::-1], jnp.bfloat16),
            pltpu.VMEM(gate_weight.shape[::-1], jnp.bfloat16),
            dma((device_total,)),
            dma((own, device_total)),
            dma((row_count, own)),
            dma((row_count, own)),
        ],
        compiler_params=pltpu.CompilerParams(
            collective_id=1, has_side_effects=True, vmem_limit_bytes=VMEM_LIMIT
        ),
        name="attention",
    )(
        carried,
        normed,
        bias_full,
        query_weight,
        key_weight,
        value_weight,
        gate_weight,
        output_weight,
    )
    pieces = pieces.reshape(row_count, tile_rows, own, channels)
    return jnp.transpose(pieces, (1, 0, 2, 3)).reshape(tile_rows, tile_cols, channels)


def per_device(pair_state, *others):
    tile_cols = pair_state.shape[1]
    row_count, col_count = lax.axis_size("row"), lax.axis_size("col")
    own = tile_cols // row_count
    if own % 8 == 0 and col_count % 2 == 0 and col_count % row_count == 0:
        return owned_columns(pair_state, *others)
    return tile_layout(pair_state, *others)


def solution(mesh):
    placed = (
        P("row", "col", None),
        P(),
        P(),
        P(),
        P(),
        P(),
        P(),
        P(),
        P(),
        P(),
        P(),
        P(),
        P(),
        P(),
    )
    return jax.shard_map(
        per_device, mesh=mesh, in_specs=placed, out_specs=P("row", "col", None), check_vma=False
    )
```

```python
import functools
import math

import jax
import jax.numpy as jnp
from jax import lax
from jax.experimental import pallas as pl
from jax.experimental.pallas import tpu as pltpu
from jax.sharding import PartitionSpec as P

MESH = pl.DeviceIdType.MESH
VMEM_LIMIT = 60 * 1024 * 1024
LOG2_E = math.log2(math.e)

mask_penalty = 1000000000.0
norm_epsilon = 1e-05


def normalize(values, gain):
    center = values - jnp.mean(values, axis=-1, keepdims=True)
    variance = jnp.mean(center * center, axis=-1, keepdims=True)
    return center * lax.rsqrt(variance + norm_epsilon) * gain


def mirror(tile):
    tile_rows, tile_cols, channels = tile.shape
    col_count = lax.axis_size("col")
    row_count = lax.axis_size("row")
    col_ratio = col_count // row_count
    piece_len = tile_cols * tile_cols // col_count
    sectioned = tile.reshape(col_ratio, col_count, piece_len, channels)
    sectioned = lax.all_to_all(sectioned, "col", split_axis=1, concat_axis=1, tiled=True)
    sectioned = sectioned.reshape(col_ratio, row_count, col_ratio, piece_len, channels)
    sectioned = lax.all_to_all(sectioned, "row", split_axis=1, concat_axis=1, tiled=True)
    sectioned = jnp.transpose(sectioned, (1, 0, 2, 3, 4)).reshape(
        col_count, col_ratio, piece_len, channels
    )
    sectioned = lax.all_to_all(sectioned, "col", split_axis=0, concat_axis=0, tiled=True)
    sectioned = jnp.transpose(sectioned, (1, 0, 2, 3)).reshape(
        col_ratio, tile_cols, tile_cols, channels
    )
    return jnp.transpose(sectioned, (0, 2, 1, 3)).reshape(tile_rows, tile_cols, channels)


def attend(query_part, gate_part, key_part, value_part, bias_part, head_count, output_weight):
    query_total = query_part.shape[0]
    key_total = key_part.shape[0]
    head_dim = query_part.shape[1] // head_count
    score_scale = 1.0 / math.sqrt(head_dim)
    query_heads = query_part.reshape(query_total, head_count, head_dim)
    key_heads = key_part.reshape(key_total, head_count, head_dim)
    value_heads = value_part.reshape(key_total, head_count, head_dim)
    scores = (
        jnp.einsum("jhd,khd->hjk", query_heads, key_heads, preferred_element_type=jnp.float32)
        * score_scale
        + bias_part
    )
    row_max = jnp.max(scores, axis=-1, keepdims=True)
    exponent = jnp.exp(scores - row_max)
    attn_weights = (exponent / jnp.sum(exponent, axis=-1, keepdims=True)).astype(jnp.bfloat16)
    mixture = jnp.einsum(
        "hjk,khd->jhd", attn_weights, value_heads, preferred_element_type=jnp.float32
    )
    gated = (gate_part * mixture.reshape(query_total, head_count * head_dim)).astype(jnp.bfloat16)
    return jnp.dot(gated, output_weight, preferred_element_type=jnp.float32).astype(jnp.bfloat16)


def mirror_layout(
    normed_tile,
    bias_tile,
    chain_ids,
    penalty,
    chain_weight,
    query_weight,
    key_weight,
    value_weight,
    gate_weight,
    output_weight,
):
    tile_rows, tile_cols, channels = normed_tile.shape
    head_count = bias_tile.shape[0]
    row_start = lax.axis_index("row") * tile_rows
    flat_tile = normed_tile.reshape(tile_rows * tile_cols, channels)
    key_tile = (
        jnp.dot(flat_tile, key_weight, preferred_element_type=jnp.float32)
        .astype(jnp.bfloat16)
        .reshape(tile_rows, tile_cols, -1)
    )
    value_tile = (
        jnp.dot(flat_tile, value_weight, preferred_element_type=jnp.float32)
        .astype(jnp.bfloat16)
        .reshape(tile_rows, tile_cols, -1)
    )
    key_all, value_all = (
        lax.all_gather(key_tile, "row", axis=0, tiled=True),
        lax.all_gather(value_tile, "row", axis=0, tiled=True),
    )
    bias_rows = lax.all_gather(bias_tile, "col", axis=2, tiled=True)
    chain_rows = lax.dynamic_slice_in_dim(chain_ids, row_start, tile_rows, 0)
    same_chain = (chain_rows[:, None] == chain_ids[None, :]).astype(jnp.float32)
    bias_full = (
        bias_rows.astype(jnp.float32)
        + chain_weight[:, None, None] * same_chain[None]
        - penalty[None, None, :]
    )
    query_tile = (
        jnp.dot(flat_tile, query_weight, preferred_element_type=jnp.float32)
        .astype(jnp.bfloat16)
        .reshape(tile_rows, tile_cols, -1)
    )
    gate_tile = jax.nn.sigmoid(
        jnp.dot(flat_tile, gate_weight, preferred_element_type=jnp.float32)
    ).reshape(tile_rows, tile_cols, -1)

    def one_column(position):
        query_part = lax.dynamic_index_in_dim(query_tile, position, 1, keepdims=False)
        gate_part = lax.dynamic_index_in_dim(gate_tile, position, 1, keepdims=False)
        key_part = lax.dynamic_index_in_dim(key_all, position, 1, keepdims=False)
        value_part = lax.dynamic_index_in_dim(value_all, position, 1, keepdims=False)
        return attend(
            query_part, gate_part, key_part, value_part, bias_full, head_count, output_weight
        )

    results = lax.map(one_column, jnp.arange(tile_cols, dtype=jnp.int32))
    return jnp.transpose(results, (1, 0, 2))


def tile_layout(
    pair_state,
    residue_mask,
    chain_ids,
    gain_transition,
    hidden_weight,
    out_weight,
    gain_attention,
    query_weight,
    key_weight,
    value_weight,
    gate_weight,
    bias_weight,
    chain_weight,
    output_weight,
):
    tile_rows, tile_cols, channels = pair_state.shape
    head_count = chain_weight.shape[0]
    mirrored = mirror(pair_state)
    sym_tile = pair_state.astype(jnp.float32) + mirrored.astype(jnp.float32)
    flat_sym = sym_tile.reshape(tile_rows * tile_cols, channels)
    first_norm = normalize(flat_sym, gain_transition).astype(jnp.bfloat16)
    hidden_act = jax.nn.relu(
        jnp.dot(first_norm, hidden_weight, preferred_element_type=jnp.float32)
    ).astype(jnp.bfloat16)
    carried = flat_sym + jnp.dot(hidden_act, out_weight, preferred_element_type=jnp.float32)
    normed = normalize(carried, gain_attention).astype(jnp.bfloat16)
    bias_tile = (
        jnp.einsum("pd,dh->hp", normed, bias_weight, preferred_element_type=jnp.float32)
        .astype(jnp.bfloat16)
        .reshape(head_count, tile_rows, tile_cols)
    )
    penalty = mask_penalty * (1 - residue_mask).astype(jnp.float32)
    normed_tile = normed.reshape(tile_rows, tile_cols, channels)
    arguments = (
        normed_tile,
        bias_tile,
        chain_ids,
        penalty,
        chain_weight,
        query_weight,
        key_weight,
        value_weight,
        gate_weight,
        output_weight,
    )
    own_update = mirror_layout(*arguments)
    other_update = mirror(own_update)
    total = (
        2.0 * carried.reshape(tile_rows, tile_cols, channels)
        + own_update.astype(jnp.float32)
        + other_update.astype(jnp.float32)
    )
    return total.astype(jnp.bfloat16)


def greet_all(row_count, col_count):
    device_total = row_count * col_count
    me = lax.axis_index("col") * row_count + lax.axis_index("row")
    barrier = pltpu.get_barrier_semaphore()

    def greet(step, carry):
        peer = lax.rem(me + step, device_total)
        pl.semaphore_signal(
            barrier,
            inc=1,
            device_id=(lax.rem(peer, row_count), peer // row_count),
            device_id_type=MESH,
        )
        return carry

    lax.fori_loop(1, device_total, greet, 0)
    pl.semaphore_wait(barrier, device_total - 1)


def transition_kernel(
    row_count,
    col_count,
    tile_ref,
    turned_ref,
    gain_transition_ref,
    hidden_weight_ref,
    out_weight_ref,
    gain_attention_ref,
    bias_weight_ref,
    carried_ref,
    normed_ref,
    bias_ref,
    row_buf,
    col_buf,
    relay_buf,
    relay_send,
    relay_recv,
    row_send,
    row_recv,
    col_send,
    col_recv,
    bias_send,
    bias_recv,
    pair_send,
    pair_recv,
):
    tile_rows, tile_cols, channels = tile_ref.shape
    own = tile_cols // row_count
    half = own // 2
    span = col_count // row_count
    chip_total = row_count * col_count // 2
    row_id, col_id = lax.axis_index("row"), lax.axis_index("col")
    me = col_id * row_count + row_id
    side = lax.rem(col_id, 2)
    chip = (col_id // 2) * row_count + row_id
    greet_all(row_count, col_count)

    def relay_copy(other, slot, part):
        return pltpu.make_async_remote_copy(
            src_ref=tile_ref.at[pl.ds((slot * row_count + other) * own + part * half, half)],
            dst_ref=relay_buf.at[row_id, slot, part],
            send_sem=relay_send.at[other, slot, part],
            recv_sem=relay_recv.at[row_id, slot, part],
            device_id=(other, col_id),
            device_id_type=MESH,
        )

    def start_rows(origin, slot, part, source):
        target = origin * span + slot
        columns = pl.ds(pl.multiple_of(col_id * tile_cols, tile_cols), tile_cols)
        landing = row_buf.at[pl.ds(part * half, half), columns, :]

        @pl.when(target != col_id)
        def _():
            pltpu.make_async_remote_copy(
                src_ref=source,
                dst_ref=landing,
                send_sem=row_send.at[origin, slot, part],
                recv_sem=row_recv.at[col_id, part],
                device_id=(row_id, target),
                device_id_type=MESH,
            ).start()

        @pl.when(target == col_id)
        def _():
            pltpu.make_async_copy(source, landing, row_recv.at[col_id, part]).start()

    def col_remote(other, part):
        return pltpu.make_async_remote_copy(
            src_ref=turned_ref.at[pl.ds(other * own + part * half, half)],
            dst_ref=col_buf.at[
                pl.ds(part * half, half), pl.ds(pl.multiple_of(row_id * tile_rows, tile_rows), tile_rows), :
            ],
            send_sem=col_send.at[other, part],
            recv_sem=col_recv.at[row_id, part],
            device_id=(other, col_id),
            device_id_type=MESH,
        )

    def over_rows(body):
        def one(step, carry):
            body(lax.rem(row_id + step, row_count))
            return carry

        lax.fori_loop(1, row_count, one, 0)

    def over_slots(body):
        def one(step, carry):
            body(lax.rem(col_id + step, span))
            return carry

        lax.fori_loop(0, span, one, 0)

    own_columns = pl.ds(pl.multiple_of(row_id * tile_rows, tile_rows), tile_rows)

    def own_col(part):
        return pltpu.make_async_copy(
            turned_ref.at[pl.ds(row_id * own + part * half, half)],
            col_buf.at[pl.ds(part * half, half), own_columns, :],
            col_recv.at[row_id, part],
        )

    def direct(slot, part):
        first = (slot * row_count + row_id) * own + part * half
        start_rows(row_id, slot, part, tile_ref.at[pl.ds(first, half)])

    def pass_on(origin, slot, part):
        arrived = relay_buf.at[origin, slot, part]
        pltpu.make_async_copy(arrived, arrived, relay_recv.at[origin, slot, part]).wait()
        start_rows(origin, slot, part, arrived)

    for part in range(2):
        over_rows(lambda other: over_slots(lambda slot: relay_copy(other, slot, part).start()))
    for part in range(2):
        over_slots(lambda slot: direct(slot, part))
        over_rows(lambda other: col_remote(other, part).start())
        own_col(part).start()
    for part in range(2):
        over_rows(lambda origin: over_slots(lambda slot: pass_on(origin, slot, part)))

    def wait_part(part):
        def wait_row(other, carry):
            columns = pl.ds(pl.multiple_of(other * tile_cols, tile_cols), tile_cols)
            landed = row_buf.at[pl.ds(part * half, half), columns, :]
            pltpu.make_async_copy(landed, landed, row_recv.at[other, part]).wait()
            return carry

        lax.fori_loop(0, col_count, wait_row, 0)

        def wait_col(other, carry):
            columns = pl.ds(pl.multiple_of(other * tile_rows, tile_rows), tile_rows)
            landed = col_buf.at[pl.ds(part * half, half), columns, :]
            pltpu.make_async_copy(landed, landed, col_recv.at[other, part]).wait()
            return carry

        lax.fori_loop(0, row_count, wait_col, 0)

    def over_chips(body):
        def one(step, carry):
            body(lax.rem(chip + step, chip_total))
            return carry

        lax.fori_loop(1, chip_total, one, 0)

    def chip_place(other, which):
        return lax.rem(other, row_count), (other // row_count) * 2 + which

    def slab(other, which):
        place = chip_place(other, which)
        return bias_ref.at[pl.ds((place[1] * row_count + place[0]) * own, own)]

    def one_row(position, carry):
        sym_row = row_buf[position].astype(jnp.float32) + col_buf[position].astype(jnp.float32)
        first_norm = normalize(sym_row, gain_transition_ref[...]).astype(jnp.bfloat16)
        hidden_act = jax.nn.relu(
            jnp.dot(first_norm, hidden_weight_ref[...], preferred_element_type=jnp.float32)
        ).astype(jnp.bfloat16)
        carried = sym_row + jnp.dot(
            hidden_act, out_weight_ref[...], preferred_element_type=jnp.float32
        )
        carried_ref[position] = carried
        normed = normalize(carried, gain_attention_ref[...]).astype(jnp.bfloat16)
        normed_ref[position] = normed
        bias_ref[me * own + position] = lax.dot_general(
            bias_weight_ref[...],
            normed,
            (((1,), (1,)), ((), ())),
            preferred_element_type=jnp.float32,
        ).astype(jnp.bfloat16)
        over_chips(
            lambda other: pltpu.make_async_remote_copy(
                src_ref=bias_ref.at[me * own + position],
                dst_ref=bias_ref.at[me * own + position],
                send_sem=bias_send.at[other],
                recv_sem=bias_recv.at[chip],
                device_id=chip_place(other, side),
                device_id_type=MESH,
            ).start()
        )
        return carry

    def part_rows(part, carry):
        wait_part(part)
        lax.fori_loop(part * half, (part + 1) * half, one_row, 0)
        return carry

    lax.fori_loop(0, 2, part_rows, 0)

    def to_pair(other):
        return pltpu.make_async_remote_copy(
            src_ref=slab(other, side),
            dst_ref=slab(other, side),
            send_sem=pair_send.at[other],
            recv_sem=pair_recv.at[other],
            device_id=(row_id, col_id + 1 - 2 * side),
            device_id_type=MESH,
        )

    to_pair(chip).start()

    def hand_over(other):
        landed = slab(other, side)
        pltpu.make_async_copy(landed, landed, bias_recv.at[other]).wait()
        to_pair(other).start()

    over_chips(hand_over)

    def close_pair(other, carry):
        landed = slab(other, 1 - side)
        pltpu.make_async_copy(landed, landed, pair_recv.at[other]).wait()
        to_pair(other).wait_send()
        return carry

    lax.fori_loop(0, chip_total, close_pair, 0)

    def close_chip(other):
        sent = slab(chip, side)
        pltpu.make_async_copy(sent, sent, bias_send.at[other]).wait()

    over_chips(close_chip)

    def close_rows(origin, slot, part):
        @pl.when(origin * span + slot != col_id)
        def _():
            sent = relay_buf.at[origin, slot, part]
            pltpu.make_async_copy(sent, sent, row_send.at[origin, slot, part]).wait()

    for part in range(2):
        over_slots(lambda slot: close_rows(row_id, slot, part))
        over_rows(lambda origin: over_slots(lambda slot: close_rows(origin, slot, part)))
        over_rows(lambda other: over_slots(lambda slot: relay_copy(other, slot, part).wait_send()))
        over_rows(lambda other: col_remote(other, part).wait_send())


def attention_kernel(
    row_count,
    col_count,
    carried_ref,
    normed_ref,
    bias_ref,
    query_weight_ref,
    key_weight_ref,
    value_weight_ref,
    gate_weight_ref,
    output_weight_ref,
    out_ref,
    total,
    update_buf,
    recv_buf,
    turned,
    sum_buf,
    score_buf,
    weight_buf,
    query_turned,
    value_turned,
    gate_turned,
    update_send,
    update_recv,
    sum_send,
    sum_recv,
):
    own, length, channels = normed_ref.shape
    head_count = bias_ref.shape[0]
    inner_total = key_weight_ref.shape[1]
    head_dim = inner_total // head_count
    score_scale = LOG2_E / math.sqrt(head_dim)
    device_total = row_count * col_count
    row_id, col_id = lax.axis_index("row"), lax.axis_index("col")
    me = col_id * row_count + row_id
    query_turned[...] = query_weight_ref[...].T
    value_turned[...] = value_weight_ref[...].T
    gate_turned[...] = gate_weight_ref[...].T
    greet_all(row_count, col_count)

    def over_peers(body):
        def one(step, carry):
            body(lax.rem(me + step, device_total))
            return carry

        lax.fori_loop(1, device_total, one, 0)

    def over_rows(body):
        def one(step, carry):
            body(lax.rem(row_id + step, row_count))
            return carry

        lax.fori_loop(1, row_count, one, 0)

    strip = min(128, length)
    band = min(inner_total, max(128, head_dim))
    heads_in_band = band // head_dim
    head_of_lane = lax.broadcasted_iota(jnp.int32, (1, band), 1) // head_dim

    def one_row(position, carry):
        normed = normed_ref[position]
        normed_turned = normed.T

        def project(weight_ref):
            return jnp.dot(weight_ref[...], normed_turned, preferred_element_type=jnp.float32)

        keys = jnp.dot(
            normed, key_weight_ref[...], preferred_element_type=jnp.float32
        ).astype(jnp.bfloat16)
        queries = project(query_turned).astype(jnp.bfloat16)
        values = project(value_turned).astype(jnp.bfloat16)
        gates = jax.nn.sigmoid(project(gate_turned))
        def score(head):
            first = head // heads_in_band * band
            chosen = (head_of_lane == head % heads_in_band).astype(jnp.bfloat16)
            score_buf[head] = (
                jnp.dot(
                    keys[:, first : first + band] * chosen,
                    queries[first : first + band],
                    preferred_element_type=jnp.float32,
                )
                * score_scale
                + bias_ref[head]
            )

        mixed = []
        for head in range(4):
            score(head)
        for head in range(head_count):
            if head + 4 < head_count:
                score(head + 4)
            rows = slice(head * head_dim, (head + 1) * head_dim)
            for start in range(0, length, strip):
                places = slice(start, start + strip)
                scores = score_buf[head, :, places]
                exponent = jnp.exp2(scores - jnp.max(scores, axis=0, keepdims=True))
                weight_buf[head, :, places] = (
                    exponent * (1.0 / jnp.sum(exponent, axis=0, keepdims=True))
                ).astype(jnp.bfloat16)
            mixture = jnp.dot(values[rows], weight_buf[head], preferred_element_type=jnp.float32)
            mixed.append((gates[rows] * mixture).astype(jnp.bfloat16))
        gated = jnp.concatenate(mixed, axis=0).T
        update = jnp.dot(gated, output_weight_ref[...], preferred_element_type=jnp.float32)
        update = update.reshape(device_total, own, channels).astype(jnp.bfloat16)
        update_buf[position] = update
        recv_buf[me, position] = update_buf[position, me]
        total[position] = 2.0 * carried_ref[position] + update.astype(jnp.float32).reshape(
            length, channels
        )
        over_peers(
            lambda peer: pltpu.make_async_remote_copy(
                src_ref=update_buf.at[position, peer],
                dst_ref=recv_buf.at[me, position],
                send_sem=update_send.at[peer],
                recv_sem=update_recv.at[position, me],
                device_id=(lax.rem(peer, row_count), peer // row_count),
                device_id_type=MESH,
            ).start()
        )
        return carry

    lax.fori_loop(0, own, one_row, 0)
    for position in range(own):
        turned[:, :, position, :] = total[position].reshape(device_total, own, channels)

    def summed(other, position):
        devices = pl.ds(other * col_count, col_count)
        return (
            turned[devices, position] + recv_buf[devices, position].astype(jnp.float32)
        ).astype(jnp.bfloat16)

    def sum_remote(other, position):
        return pltpu.make_async_remote_copy(
            src_ref=sum_buf.at[other, :, position],
            dst_ref=out_ref.at[row_id, :, position],
            send_sem=sum_send.at[other, position],
            recv_sem=sum_recv.at[row_id, position],
            device_id=(other, col_id),
            device_id_type=MESH,
        )

    def finish_position(position, carry):
        def arrived(peer):
            landed = recv_buf.at[peer, position]
            pltpu.make_async_copy(landed, landed, update_recv.at[position, peer]).wait()

        over_peers(arrived)

        def pass_sum(other):
            sum_buf[other, :, position] = summed(other, position)
            sum_remote(other, position).start()

        over_rows(pass_sum)
        out_ref[row_id, :, position] = summed(row_id, position)
        return carry

    lax.fori_loop(0, own, finish_position, 0)

    def close_peer(peer):
        sent = recv_buf.at[peer]
        pltpu.make_async_copy(sent, sent, update_send.at[peer]).wait()

    over_peers(close_peer)

    def close_position(position, carry):
        def close_row(other):
            landed = out_ref.at[other, :, position]
            pltpu.make_async_copy(landed, landed, sum_recv.at[other, position]).wait()
            sum_remote(other, position).wait_send()

        over_rows(close_row)
        return carry

    lax.fori_loop(0, own, close_position, 0)


def owned_columns(
    pair_state,
    residue_mask,
    chain_ids,
    gain_transition,
    hidden_weight,
    out_weight,
    gain_attention,
    query_weight,
    key_weight,
    value_weight,
    gate_weight,
    bias_weight,
    chain_weight,
    output_weight,
):
    tile_rows, tile_cols, channels = pair_state.shape
    row_count, col_count = lax.axis_size("row"), lax.axis_size("col")
    device_total = row_count * col_count
    head_count = chain_weight.shape[0]
    length = tile_rows * row_count
    own = tile_cols // row_count
    span = col_count // row_count
    in_vmem = pl.BlockSpec(memory_space=pltpu.VMEM)
    dma = pltpu.SemaphoreType.DMA
    carried, normed, bias_rows = pl.pallas_call(
        functools.partial(transition_kernel, row_count, col_count),
        out_shape=(
            jax.ShapeDtypeStruct((own, length, channels), jnp.float32),
            jax.ShapeDtypeStruct((own, length, channels), jnp.bfloat16),
            jax.ShapeDtypeStruct((length, head_count, length), jnp.bfloat16),
        ),
        in_specs=[in_vmem] * 7,
        out_specs=(in_vmem,) * 3,
        scratch_shapes=[
            pltpu.VMEM((own, length, channels), jnp.bfloat16),
            pltpu.VMEM((own, length, channels), jnp.bfloat16),
            pltpu.VMEM((row_count, span, 2, own // 2, tile_cols, channels), jnp.bfloat16),
            dma((row_count, span, 2)),
            dma((row_count, span, 2)),
            dma((row_count, span, 2)),
            dma((col_count, 2)),
            dma((row_count, 2)),
            dma((row_count, 2)),
            dma((device_total // 2,)),
            dma((device_total // 2,)),
            dma((device_total // 2,)),
            dma((device_total // 2,)),
        ],
        compiler_params=pltpu.CompilerParams(
            collective_id=0, has_side_effects=True, vmem_limit_bytes=VMEM_LIMIT
        ),
        name="transition",
    )(
        pair_state,
        jnp.transpose(pair_state, (1, 0, 2)),
        gain_transition[None, :],
        hidden_weight,
        out_weight,
        gain_attention[None, :],
        bias_weight.T,
    )
    penalty = mask_penalty * (1 - residue_mask).astype(jnp.float32)
    same_chain = (chain_ids[:, None] == chain_ids[None, :]).astype(jnp.float32)
    bias_full = (
        jnp.transpose(bias_rows, (1, 0, 2)).astype(jnp.float32)
        + chain_weight[:, None, None] * same_chain[None]
        - penalty[None, :, None]
    ) * LOG2_E
    pieces = pl.pallas_call(
        functools.partial(attention_kernel, row_count, col_count),
        out_shape=jax.ShapeDtypeStruct((row_count, col_count, own, own, channels), jnp.bfloat16),
        in_specs=[in_vmem] * 8,
        out_specs=in_vmem,
        scratch_shapes=[
            pltpu.VMEM((own, length, channels), jnp.float32),
            pltpu.VMEM((own, device_total, own, channels), jnp.bfloat16),
            pltpu.VMEM((device_total, own, own, channels), jnp.bfloat16),
            pltpu.VMEM((device_total, own, own, channels), jnp.float32),
            pltpu.VMEM((row_count, col_count, own, own, channels), jnp.bfloat16),
            pltpu.VMEM((head_count, length, length), jnp.float32),
            pltpu.VMEM((head_count, length, length), jnp.bfloat16),
            pltpu.VMEM(query_weight.shape[::-1], jnp.bfloat16),
            pltpu.VMEM(value_weight.shape[::-1], jnp.bfloat16),
            pltpu.VMEM(gate_weight.shape[::-1], jnp.bfloat16),
            dma((device_total,)),
            dma((own, device_total)),
            dma((row_count, own)),
            dma((row_count, own)),
        ],
        compiler_params=pltpu.CompilerParams(
            collective_id=1, has_side_effects=True, vmem_limit_bytes=VMEM_LIMIT
        ),
        name="attention",
    )(
        carried,
        normed,
        bias_full,
        query_weight,
        key_weight,
        value_weight,
        gate_weight,
        output_weight,
    )
    pieces = pieces.reshape(row_count, tile_rows, own, channels)
    return jnp.transpose(pieces, (1, 0, 2, 3)).reshape(tile_rows, tile_cols, channels)


def per_device(pair_state, *others):
    tile_cols = pair_state.shape[1]
    row_count, col_count = lax.axis_size("row"), lax.axis_size("col")
    own = tile_cols // row_count
    if own % 8 == 0 and col_count % 2 == 0 and col_count % row_count == 0:
        return owned_columns(pair_state, *others)
    return tile_layout(pair_state, *others)


def solution(mesh):
    placed = (
        P("row", "col", None),
        P(),
        P(),
        P(),
        P(),
        P(),
        P(),
        P(),
        P(),
        P(),
        P(),
        P(),
        P(),
        P(),
    )
    return jax.shard_map(
        per_device, mesh=mesh, in_specs=placed, out_specs=P("row", "col", None), check_vma=False
    )
```
